32 devices in a mesh: row: 8 (over y, x, core), col: 4 (over z).
Axes of the slice: x: 2, y: 2, z: 4, core: 2. Of those that a mesh axis runs over, the one named last changes fastest.
Arguments:
- sweep_start: int32 [8], replicated, may hold values from 1 to 63, as said below
- block_len: int32 [8, 32], P(None, 'row'), may hold values from 64 to 128, as said below
- reflectors: float32 [8, 32, 128, 64], P('col', 'row'), may hold values from -8 to 8, as said below
- tfactors: float32 [8, 32, 64, 64], P('col', 'row'), may hold values from -2 to 2, as said below
- panel: float32 [4096, 128], P('row'), may hold values from -180 to 180
- eigvecs: float32 [4096, 2048], P('row', 'col'), may hold values from -4 to 4
Outputs:
- result: float32 [4096, 2048], P('row', 'col')
The draws below stay inside these ranges and needn't reach their ends.
Inputs may be any that keep to these rules, and one draw needn't show every extreme that they name: `sweep_start`: some sweep starts at row 63. In the last block of each sweep, sweep_start plus block_len is at most 128. `reflectors`: each block's vectors are unit lower trapezoidal: entry (k, k) is 1 and entries above it are 0. tfactors[s, b] is the triangular factor that makes the block a product of Householder reflections of its masked vectors.
All inputs are finite; a program needn't handle non-finite values.
Results may differ from the reference program's by a relative error of at most 0.0003.
Values sent between devices are 32-bit elements; how exact they have to be, the bound alone decides.
A program may use at most 64 MiB of HBM per device.

```python
import jax
import jax.numpy as jnp
from jax import lax

ROWS = 512
BAND = 128
KREF = 64
WANTED = 2048
SWEEPS = 8
ORDER = 4096
N_ROW = 8


def sweep_layout(key):
    base = jax.random.fold_in(key, 11)
    key_start, key_widest, key_length, key_device = jax.random.split(base, 4)
    block_total = ROWS // BAND * N_ROW
    starts = jax.random.randint(key_start, (SWEEPS,), 1, BAND // 2)
    widest = jax.random.randint(key_widest, (), 0, SWEEPS)
    sweep_ids = jnp.arange(SWEEPS)
    starts = jnp.where(sweep_ids == widest, BAND // 2 - 1, starts)
    lengths = jax.random.randint(key_length, (SWEEPS, block_total), KREF, BAND + 1)
    device = jax.random.randint(key_device, (), 0, N_ROW - 1)
    target = device * (ROWS // BAND) + ROWS // BAND - 1
    block_ids = jnp.arange(block_total)
    hit = (sweep_ids[:, None] == widest) & (block_ids[None, :] == target)
    lengths = jnp.where(hit, BAND, lengths)
    capped = jnp.minimum(lengths[:, block_total - 1], BAND - starts)
    lengths = lengths.at[:, block_total - 1].set(capped)
    return (starts.astype(jnp.int32), lengths.astype(jnp.int32))


def invert_batch(upper):
    width = upper.shape[-1]
    diagonal = jnp.diagonal(upper, axis1=-2, axis2=-1)
    scaled = upper / diagonal[..., :, None]
    identity = jnp.eye(width, dtype=jnp.float32)
    strict = scaled - identity
    solved = jnp.zeros_like(upper)

    def sweep_row(counter, current):
        row_id = width - 1 - counter
        strict_row = lax.dynamic_slice_in_dim(strict, row_id, 1, axis=strict.ndim - 2)
        unit_row = lax.dynamic_slice_in_dim(identity, row_id, 1, axis=0)
        known = jnp.einsum('...ij,...jk->...ik', strict_row, current, precision=lax.Precision.HIGHEST)
        new_row = unit_row - known
        return lax.dynamic_update_slice_in_dim(current, new_row, row_id, axis=current.ndim - 2)
    solved = lax.fori_loop(0, width, sweep_row, solved)
    return solved / diagonal[..., None, :]


def reflector_set(key):
    starts, lengths = sweep_layout(key)
    block_total = ROWS // BAND * N_ROW
    key_values = jax.random.fold_in(jax.random.fold_in(key, 23), 0)
    shape = (SWEEPS, block_total, BAND, KREF)
    values = 0.5 * jax.random.truncated_normal(key_values, -4.0, 4.0, shape, jnp.float32)
    row_ids = jnp.arange(BAND)[:, None]
    col_ids = jnp.arange(KREF)[None, :]
    below = (row_ids > col_ids).astype(jnp.float32)
    diagonal = (row_ids == col_ids).astype(jnp.float32)
    norm_scale = lax.rsqrt(lengths.astype(jnp.float32))[:, :, None, None]
    values = values * norm_scale * below + diagonal
    row_mask = (jnp.arange(BAND)[None, None, :] < lengths[:, :, None]).astype(jnp.float32)
    masked = values * row_mask[..., None]
    gram = jnp.einsum('sjbk,sjbl->sjkl', masked, masked, precision=lax.Precision.HIGHEST)
    identity = jnp.eye(KREF, dtype=jnp.float32)
    upper_form = jnp.triu(gram, 1) + 0.5 * gram * identity
    factors = invert_batch(upper_form)
    return (values, factors)


def vector_set(key):
    base = jax.random.fold_in(key, 37)
    key_vectors, key_noise, key_columns, key_scale = jax.random.split(base, 4)
    vectors = jax.random.truncated_normal(key_vectors, -4.0, 4.0, (ORDER, WANTED), jnp.float32)
    spread = 10.0
    columns = jax.random.permutation(key_columns, WANTED)[:BAND]
    noise = jax.random.truncated_normal(key_noise, -4.0, 4.0, (ORDER, BAND), jnp.float32)
    scales = jnp.exp(jax.random.uniform(key_scale, (ORDER, 1), jnp.float32, 0.0, jnp.log(spread)))
    panel = (vectors[:, columns] + 0.5 * noise) * scales
    return (vectors, panel)


def draw_sweep_start(key, part):
    return sweep_layout(key)[0]


def draw_block_len(key, part):
    return sweep_layout(key)[1]


def draw_reflectors(key, part):
    return reflector_set(key)[0]


def draw_tfactors(key, part):
    return reflector_set(key)[1]


def draw_panel(key, part):
    return vector_set(key)[1]


def draw_eigvecs(key, part):
    return vector_set(key)[0]


def setup_inputs(seed: int = 0) -> dict:
    seeds = jax.random.split(jax.random.key(seed), 7)
    return {
        "sweep_start": draw_sweep_start(jax.random.fold_in(seeds[6], 71), 0),
        "block_len": draw_block_len(jax.random.fold_in(seeds[6], 71), 0),
        "reflectors": draw_reflectors(jax.random.fold_in(seeds[6], 71), 0),
        "tfactors": draw_tfactors(jax.random.fold_in(seeds[6], 71), 0),
        "panel": draw_panel(jax.random.fold_in(seeds[6], 71), 0),
        "eigvecs": draw_eigvecs(jax.random.fold_in(seeds[6], 71), 0),
    }


def apply_blocks(window, reflect, triangle):
    highest = lax.Precision.HIGHEST
    projected = jnp.einsum('jbk,jbm->jkm', reflect, window, precision=highest)
    combined = jnp.einsum('jkl,jlm->jkm', triangle, projected, precision=highest)
    return window - jnp.einsum('jbk,jkm->jbm', reflect, combined, precision=highest)

def reference(sweep_start, block_len, reflectors, tfactors, panel, eigvecs):
    highest = lax.Precision.HIGHEST
    block_total = ORDER // BAND
    lane_index = jnp.arange(BAND, dtype=jnp.int32)
    vectors = eigvecs
    for step_index in range(SWEEPS):
        padded = jnp.concatenate([vectors, jnp.zeros((BAND, WANTED), eigvecs.dtype)], axis=0)
        offset = sweep_start[step_index].astype(jnp.int32)
        window = lax.dynamic_slice_in_dim(padded, offset, ORDER, 0).reshape(block_total, BAND, WANTED)
        live_rows = (lane_index[None, :] < block_len[step_index][:, None]).astype(eigvecs.dtype)
        masked = reflectors[step_index] * live_rows[:, :, None]
        window = apply_blocks(window, masked, tfactors[step_index])
        padded = lax.dynamic_update_slice_in_dim(padded, window.reshape(ORDER, WANTED), offset, 0)
        vectors = padded[:ORDER]
    gram_total = lax.dot_general(panel, panel, (((0,), (0,)), ((), ())), precision=highest)
    projection = lax.dot_general(panel, vectors, (((0,), (0,)), ((), ())), precision=highest)
    identity = jnp.eye(BAND, dtype=panel.dtype)
    upper_form = jnp.triu(gram_total, 1) + 0.5 * gram_total * identity
    factor = lax.linalg.triangular_solve(upper_form, identity, left_side=True, lower=False)
    inner = jnp.dot(factor, projection, precision=highest)
    return vectors - jnp.dot(panel, inner, precision=highest)
```

```python
import functools

import jax
import jax.numpy as jnp
from jax import lax
from jax.experimental import pallas as pl
from jax.experimental.pallas import tpu as pltpu
from jax.sharding import PartitionSpec as P

MESH = pl.DeviceIdType.MESH
LANES = 128
GROUPS = 4


def split(value):
    high = value.astype(jnp.bfloat16)
    return high, (value - high.astype(jnp.float32)).astype(jnp.bfloat16)


def mm(left, right):
    return jnp.dot(left, right, preferred_element_type=jnp.float32)


def mm_nt(left, right):
    return lax.dot_general(left, right, (((1,), (1,)), ((), ())), preferred_element_type=jnp.float32)


def three(product, left, right):
    (lh, ll), (rh, rl) = split(left), split(right)
    return product(lh, rh) + product(lh, rl) + product(ll, rh)


def wide_left(value):
    high, low = split(value)
    return jnp.concatenate([high, low, high], axis=1)


def tall_right(value):
    high, low = split(value)
    return jnp.concatenate([high, high, low], axis=0)


def kernel(
    sizes, start_ref, len_ref, reflect_hbm, factor_hbm, panel_hbm, eig_ref, out_ref, *scratch
):
    n, nc, sweeps, owned, blocks, band, width, rows, slices = sizes
    half = band // 2
    chunks = eig_ref.shape[1] // LANES
    per_group = chunks // GROUPS
    group_cols = per_group * LANES
    slice_rows = band // slices
    first, middle_end = 2 * half, 2 * half + rows

    count = (sweeps + 1) * GROUPS
    exts, scratch = scratch[:count], scratch[count:]
    (reflect_ref, factor_ref, panel_ref, early, load_sem, packed, pt, gram_out, gram_in, gram_full, proj_out, proj_in, proj_full,
     up_out, up_in, down_out, down_in, known_up, known_down,
     head_out, head_in, tail_out, tail_in, corner_sems,
     eig_sem, up_send, up_recv, down_send, down_recv,
     right_send, left_send, piece_recv, sum_sems) = scratch

    me = lax.axis_index("row")
    z = lax.axis_index("col")

    def ext(t, g):
        return exts[t * GROUPS + g]

    barrier = pltpu.get_barrier_semaphore()
    for k in range(1, n):
        pl.semaphore_signal(barrier, inc=1, device_id={"row": lax.rem(me + k, n)}, device_id_type=MESH)
    for k in range(1, nc):
        pl.semaphore_signal(barrier, inc=1, device_id={"col": lax.rem(z + k, nc)}, device_id_type=MESH)

    block_loads = [
        pltpu.make_async_copy(reflect_hbm, reflect_ref, load_sem.at[0]),
        pltpu.make_async_copy(factor_hbm, factor_ref, load_sem.at[1]),
    ]
    panel_load = pltpu.make_async_copy(panel_hbm, panel_ref.at[half:half + rows], load_sem.at[2])
    for copy in block_loads:
        copy.start()
    loads = []
    for c in range(chunks):
        g, i = divmod(c, per_group)
        copy = pltpu.make_async_copy(
            eig_ref.at[:, c * LANES:(c + 1) * LANES],
            ext(0, g).at[i, first:middle_end],
            eig_sem.at[c],
        )
        copy.start()
        loads.append(copy)
    panel_load.start()

    flat_row = lax.broadcasted_iota(jnp.int32, (width, band), 0)
    flat_col = lax.broadcasted_iota(jnp.int32, (width, band), 1)
    right_of = flat_col > flat_row
    unit = (flat_col == flat_row).astype(jnp.float32)
    for copy in block_loads:
        copy.wait()
    for i in range(owned):
        for b in range(blocks):
            turned = jnp.transpose(factor_ref[i, b])
            turned = jnp.concatenate([turned, jnp.zeros((width, band - width), jnp.float32)], axis=1)
            packed[z * owned + i, b] = jnp.where(right_of, reflect_ref[i, b], turned)

    zeros = jnp.zeros((half, LANES), jnp.float32)
    turns = sweeps // 2 + 1

    @pl.when(me == 0)
    def _():
        panel_ref[:half] = zeros
        tail_in[...] = jnp.zeros_like(tail_in)
        for t in range(sweeps + 1):
            for g in range(GROUPS):
                for i in range(per_group):
                    ext(t, g)[i, :half] = zeros
                    if t == 0:
                        ext(t, g)[i, half:first] = zeros

    @pl.when(me == n - 1)
    def _():
        panel_ref[half + rows:] = zeros
        head_in[...] = jnp.zeros_like(head_in)
        for turn in range(turns):
            for g in range(GROUPS):
                for i in range(per_group):
                    up_in[turn, g, i] = zeros

    pl.semaphore_wait(barrier, n - 1 + nc - 1)

    def piece(s, b, to_right):
        sems = right_send if to_right else left_send
        return pltpu.make_async_remote_copy(
            packed.at[s, b], packed.at[s, b], sems.at[s, b], piece_recv.at[s, b],
            device_id={"col": z + 1 if to_right else z - 1}, device_id_type=MESH,
        )

    def send_own(i, to_right):
        for b in range(blocks):
            piece_copy = pltpu.make_async_remote_copy(
                packed.at[z * owned + i, b], packed.at[z * owned + i, b],
                (right_send if to_right else left_send).at[z * owned + i, b],
                piece_recv.at[z * owned + i, b],
                device_id={"col": z + 1 if to_right else z - 1}, device_id_type=MESH,
            )
            piece_copy.start()

    @pl.when(z == 0)
    def _():
        for i in range(owned):
            send_own(i, True)

    @pl.when(jnp.logical_and(z > 0, z < nc - 1))
    def _():
        send_own(0, True)

    @pl.when(z > 0)
    def _():
        for i in range(owned):
            send_own(i, False)

    forwards = {}
    waited_early = {}
    for s in range(sweeps):
        origin = s // owned
        for where in range(origin + 1, nc - 1):
            step = 0 if s < owned else s - 1
            forwards.setdefault(step, []).append((s, where, True))
            waited_early.setdefault(s, []).append(where)
        for where in range(1, origin):
            step = min(s, s % owned + 1 + owned * (origin - where - 1))
            forwards.setdefault(step, []).append((s, where, False))
            waited_early.setdefault(s, []).append(where)

    def gather_step(t):
        for s, where, to_right in forwards.get(t, []):
            @pl.when(z == where)
            def _():
                for b in range(blocks):
                    copy = piece(s, b, to_right)
                    copy.wait_recv()
                    copy.start()
        if t % 2 == 1:
            mine = (t + 1) // 2
            if mine < nc - 1:
                @pl.when(z == mine)
                def _():
                    for i in range(1, owned):
                        send_own(i, True)
        keep = z != t // owned
        for where in waited_early.get(t, []):
            keep = jnp.logical_and(keep, z != where)

        @pl.when(keep)
        def _():
            for b in range(blocks):
                pltpu.make_async_copy(packed.at[t, b], packed.at[t, b], piece_recv.at[t, b]).wait()

    def finish_gather():
        for s in range(sweeps):
            origin = s // owned

            @pl.when(jnp.logical_and(z >= origin, z < nc - 1))
            def _():
                for b in range(blocks):
                    piece(s, b, True).wait_send()

            @pl.when(jnp.logical_and(z <= origin, z > 0))
            def _():
                for b in range(blocks):
                    piece(s, b, False).wait_send()

    def up_copy(t, g):
        turn = (t + 1) // 2
        source = ext(0, g).at[:, first:first + half] if t == 0 else up_out.at[turn, g]
        return pltpu.make_async_remote_copy(
            source, up_in.at[turn, g],
            up_send.at[turn, g], up_recv.at[turn, g], device_id={"row": me - 1}, device_id_type=MESH,
        )

    def down_copy(t, g):
        turn = (t + 1) // 2
        return pltpu.make_async_remote_copy(
            down_out.at[turn, g], down_in.at[turn, g],
            down_send.at[turn, g], down_recv.at[turn, g], device_id={"row": me + 1}, device_id_type=MESH,
        )

    def head_copy(t):
        turn = (t + 1) // 2
        return pltpu.make_async_remote_copy(
            head_out.at[turn], head_in.at[turn], corner_sems.at[turn, 0], corner_sems.at[turn, 1],
            device_id={"row": me - 1}, device_id_type=MESH,
        )

    def tail_copy(t):
        turn = (t + 1) // 2
        return pltpu.make_async_remote_copy(
            tail_out.at[turn], tail_in.at[turn], corner_sems.at[turn, 2], corner_sems.at[turn, 3],
            device_id={"row": me + 1}, device_id_type=MESH,
        )

    def halo_start(t, g):
        @pl.when(me > 0)
        def _():
            up_copy(t, g).start()
        if t > 0:
            @pl.when(me < n - 1)
            def _():
                down_copy(t, g).start()

    def halo_take(t, g):
        turn = (t + 1) // 2
        here = ext(t, g)

        @pl.when(me < n - 1)
        def _():
            up_copy(t, g).wait_recv()

        for i in range(per_group):
            here[i, middle_end:middle_end + half] = up_in[turn, g, i]
        if t > 0:
            @pl.when(me > 0)
            def _():
                down_copy(t, g).wait_recv()
                for i in range(per_group):
                    here[i, half:first] = down_in[turn, g, i]

    def finish_halo():
        for t in [0] + list(range(1, sweeps, 2)):
            for g in range(GROUPS):
                @pl.when(me > 0)
                def _():
                    up_copy(t, g).wait_send()
                if t > 0:
                    @pl.when(me < n - 1)
                    def _():
                        down_copy(t, g).wait_send()
            if t > 0:
                if t < sweeps - 1:
                    @pl.when(me > 0)
                    def _():
                        head_copy(t).wait_send()

                @pl.when(me < n - 1)
                def _():
                    tail_copy(t).wait_send()

    def owner_only(owner, run):
        if slices == n:
            run()
        else:
            pl.when(owner < slices)(run)

    def owners_differ(refs, sem):
        def wait(many):
            view = refs.at[pl.ds(0, many)]
            pltpu.make_async_copy(view, view, sem).wait()

        if slices == n:
            wait(slices - 1)
        else:
            pl.when(me < slices)(lambda: wait(slices - 1))
            pl.when(me >= slices)(lambda: wait(slices))

    def scatter_start(out, into, base):
        for k in range(1, n):
            peer = lax.rem(me + k, n)

            def run():
                pltpu.make_async_remote_copy(
                    out.at[peer], into.at[n - k - 1], sum_sems.at[base], sum_sems.at[base + 1],
                    device_id={"row": peer}, device_id_type=MESH,
                ).start()

            owner_only(peer, run)

    def reduce_and_spread(out, into, full, base):
        def run():
            pltpu.make_async_copy(into, into, sum_sems.at[base + 1]).wait()
            total = out[me]
            for k in range(n - 1):
                total = total + into[k]
            full[me] = total
            for k in range(1, n):
                pltpu.make_async_remote_copy(
                    full.at[me], full.at[me], sum_sems.at[base + 2], sum_sems.at[base + 3],
                    device_id={"row": lax.rem(me + k, n)}, device_id_type=MESH,
                ).start()

        owner_only(me, run)

    def spread_wait(full, base):
        owners_differ(full, sum_sems.at[base + 3])

    def finish_sum(out, into, base):
        owners_differ(out, sum_sems.at[base])

        def run():
            pltpu.make_async_copy(into, into, sum_sems.at[base + 2]).wait()

        owner_only(me, run)

    for copy in loads:
        copy.wait()
    for g in range(GROUPS):
        halo_start(0, g)

    panel_load.wait()
    panel_up = pltpu.make_async_remote_copy(
        panel_ref.at[half:2 * half], panel_ref.at[half + rows:2 * half + rows],
        load_sem.at[3], load_sem.at[4], device_id={"row": me - 1}, device_id_type=MESH,
    )

    @pl.when(me > 0)
    def _():
        panel_up.start()

    transposed = jnp.transpose(panel_ref[half:half + rows])
    for b in range(blocks):
        pt[b] = wide_left(transposed[:, b * band:(b + 1) * band])
    gram = mm(pt[0], tall_right(panel_ref[half:half + band]))
    for b in range(1, blocks):
        gram = gram + mm(pt[b], tall_right(panel_ref[half + b * band:half + (b + 1) * band]))
    for k in range(slices):
        gram_out[k] = gram[k * slice_rows:(k + 1) * slice_rows]
    scatter_start(gram_out, gram_in, 0)

    highest = lax.Precision.HIGHEST
    row_id = lax.broadcasted_iota(jnp.int32, (band, band), 0)
    col_id = lax.broadcasted_iota(jnp.int32, (band, band), 1)
    identity = (row_id == col_id).astype(jnp.float32)
    state = {}

    def factor_start():
        spread_wait(gram_full, 0)
        total = jnp.concatenate([gram_full[k] for k in range(slices)], axis=0)
        diagonal = 0.5 * total * identity
        state["by_col"] = jnp.sum(diagonal, axis=0, keepdims=True)
        by_row = jnp.sum(diagonal, axis=1, keepdims=True)
        state["power"] = jnp.where(row_id < col_id, total, 0.0) / by_row
        state["inverse"] = identity - state["power"]
        state["reach"] = 1

    def factor_more():
        if state["reach"] * 2 < band:
            state["power"] = jnp.dot(
                state["power"], state["power"], precision=highest, preferred_element_type=jnp.float32
            )
            state["inverse"] = jnp.dot(
                state["inverse"], identity + state["power"],
                precision=highest, preferred_element_type=jnp.float32,
            )
            state["reach"] *= 2

    def offset(t):
        return start_ref[t] if 0 <= t < sweeps else 0

    def delta(t):
        return offset(t) - offset(t - 1)

    def take(ref, at, many):
        return jnp.concatenate([ref[i, pl.ds(at, many), :] for i in range(per_group)], axis=1)

    def put(ref, at, value):
        for i in range(per_group):
            ref[i, at:at + value.shape[0]] = value[:, i * LANES:(i + 1) * LANES]

    band_row = lax.broadcasted_iota(jnp.int32, (band, group_cols), 0)
    half_row = lax.broadcasted_iota(jnp.int32, (half, group_cols), 0)
    squares = {}
    corners = {}

    def prepare(t):
        gather_step(t)
        plain = []
        squares[t] = []
        for b in range(blocks):
            pack = packed[t, b]
            flat = jnp.where(right_of, pack, unit)
            flat = jnp.where(flat_col < len_ref[b, t], flat, 0.0)
            turned = jnp.where(right_of, 0.0, pack)[:, :width]
            scaled = three(mm_nt, jnp.transpose(flat), turned)
            square = three(mm, scaled, flat)
            plain.append(square)
            squares[t].append(wide_left(square))
            if t == sweeps - 1:
                if b == 0:
                    @pl.when(me < n - 1)
                    def _():
                        panel_up.wait_recv()
                side = jnp.transpose(panel_ref[pl.ds(half + b * band + start_ref[t], band), :])
                early[b] = wide_left(side - mm(wide_left(side), tall_right(square)))
        if t % 2 == 1:
            turn = (t + 1) // 2
            quarter = half // 2

            def fold(corner):
                return jnp.concatenate([corner[:quarter], corner[quarter:]], axis=1)

            if t < sweeps - 1:
                head_out[turn] = fold((identity - plain[0])[:half, :half])

                @pl.when(me > 0)
                def _():
                    head_copy(t).start()
            tail_out[turn] = fold((identity - plain[-1])[half:, half:])

            @pl.when(me < n - 1)
            def _():
                tail_copy(t).start()

    def corner_take(t):
        turn = (t + 1) // 2

        def unfold(both):
            return wide_left(jnp.concatenate([both[:, :half], both[:, half:]], axis=0))

        if t < sweeps - 1:
            @pl.when(me < n - 1)
            def _():
                head_copy(t).wait_recv()
            corners[t, 0] = unfold(head_in[turn])

        @pl.when(me > 0)
        def _():
            tail_copy(t).wait_recv()
        corners[t, 1] = unfold(tail_in[turn])

    def send_ahead(t, g):
        turn = (t + 1) // 2
        here = ext(t, g)
        move = delta(t)
        down_by, up_by = jnp.maximum(move, 0), jnp.maximum(-move, 0)
        top = take(here, first, half)
        if t < sweeps - 1:
            window = take(here, first + move, band)
            window = jnp.where(band_row + move >= 0, window, 0.0)
            put(known_up.at[g], half, window[:half] - mm(squares[t][0][:half], tall_right(window)))
            top = jnp.where(half_row < down_by, top, take(known_up.at[g], half - down_by, half))
        put(up_out.at[turn, g], 0, top)
        window = take(here, first + (blocks - 1) * band + move, band)
        window = jnp.where(band_row + move < band, window, 0.0)
        put(known_down.at[g], 0, window[half:] - mm(squares[t][-1][half:], tall_right(window)))
        low = jnp.where(
            half_row >= half - up_by, take(here, middle_end - half, half), take(known_down.at[g], up_by, half)
        )
        put(down_out.at[turn, g], 0, low)
        halo_start(t, g)

    def sweep(t, g):
        here, after = ext(t, g), ext(t + 1, g)
        move = delta(t)
        total = None
        for b in range(blocks):
            window = take(here, first + b * band + move, band)
            tall = tall_right(window)
            if t == sweeps - 1:
                term = mm(early[b], tall)
                total = term if total is None else total + term
            put(after, first + b * band, window - mm(squares[t][b], tall))
        if t % 2 == 1:
            shift = jnp.where(me == 0, move, jnp.minimum(move, 0))
            lead = jnp.where(half_row >= half - move, take(here, first + move - half, half), 0.0)
            put(after, half, take(here, half + shift, half) + mm(corners[t, 1], tall_right(lead)))
            if t < sweeps - 1:
                rest = jnp.where(half_row < -move, take(here, middle_end + move, half), 0.0)
                put(
                    after, middle_end,
                    take(here, middle_end + jnp.maximum(move, 0), half) + mm(corners[t, 0], tall_right(rest)),
                )
        else:
            @pl.when(me == 0)
            def _():
                put(after, half, take(here, half + move, half))
        if t == sweeps - 1:
            for k in range(slices):
                proj_out[g, k] = total[k * slice_rows:(k + 1) * slice_rows]

            @pl.when(me == 0)
            def _():
                side = jnp.transpose(panel_ref[pl.ds(start_ref[t], half), :])
                more = three(mm, side, take(here, half + move, half))
                for k in range(slices):
                    proj_out[g, k] = proj_out[g, k] + more[k * slice_rows:(k + 1) * slice_rows]

            scatter_start(proj_out.at[g], proj_in.at[g], 4 + 4 * g)

    prepare(0)
    for g in range(GROUPS):
        halo_take(0, g)
        sweep(0, g)
    for t in range(1, sweeps, 2):
        prepare(t)
        for g in range(GROUPS):
            send_ahead(t, g)
        if t + 1 < sweeps:
            prepare(t + 1)
        if t == 3:
            reduce_and_spread(gram_out, gram_in, gram_full, 0)
        if t == 5:
            factor_start()
        if t >= 5:
            for _ in range(4):
                factor_more()
        corner_take(t)
        for g in range(GROUPS):
            halo_take(t, g)
            sweep(t, g)
        if t + 1 < sweeps:
            for g in range(GROUPS):
                sweep(t + 1, g)

    for g in range(GROUPS):
        columns = slice(g * group_cols, (g + 1) * group_cols)
        here = ext(sweeps, g)
        for b in range(blocks):
            out_ref[b * band:(b + 1) * band, columns] = take(here, first + b * band + delta(sweeps), band)
        reduce_and_spread(proj_out.at[g], proj_in.at[g], proj_full.at[g], 4 + 4 * g)
    while state["reach"] * 2 < band:
        factor_more()

    factor = wide_left(state["inverse"] / state["by_col"])
    for g in range(GROUPS):
        columns = slice(g * group_cols, (g + 1) * group_cols)
        spread_wait(proj_full.at[g], 4 + 4 * g)
        projection = jnp.concatenate([proj_full[g, k] for k in range(slices)], axis=0)
        inner = tall_right(mm(factor, tall_right(projection)))
        for b in range(blocks):
            part = slice(b * band, (b + 1) * band)
            out_ref[part, columns] = out_ref[part, columns] - mm(wide_left(panel_ref[half + b * band:half + (b + 1) * band]), inner)

    @pl.when(me > 0)
    def _():
        panel_up.wait_send()

    finish_gather()
    finish_halo()
    finish_sum(gram_out, gram_in, 0)
    for g in range(GROUPS):
        finish_sum(proj_out.at[g], proj_in.at[g], 4 + 4 * g)


def body(sweep_start, block_len, reflectors, tfactors, panel, eigvecs):
    rows, cols = eigvecs.shape
    owned, blocks, band, width = reflectors.shape
    flat = jnp.swapaxes(reflectors, 2, 3)
    n, nc = lax.axis_size("row"), lax.axis_size("col")
    sweeps = owned * nc
    slices = min(n, band // 8)
    part = band // slices
    chunks = cols // LANES
    group_cols = cols // GROUPS
    turns = sweeps // 2 + 1
    sizes = (n, nc, sweeps, owned, blocks, band, width, rows, slices)
    vmem = pl.BlockSpec(memory_space=pltpu.VMEM)
    smem = pl.BlockSpec(memory_space=pltpu.SMEM)
    f32 = jnp.float32
    dma = pltpu.SemaphoreType.DMA
    scratch = [
        pltpu.VMEM((chunks // GROUPS, rows + 4 * (band // 2), LANES), f32)
        for _ in range((sweeps + 1) * GROUPS)
    ] + [
        pltpu.VMEM((owned, blocks, width, band), f32),
        pltpu.VMEM((owned, blocks, width, width), f32),
        pltpu.VMEM((rows + 2 * (band // 2), band), f32),
        pltpu.VMEM((blocks, band, 3 * band), jnp.bfloat16),
        dma((5,)),
        pltpu.VMEM((sweeps, blocks, width, 2 * width), f32),
        pltpu.VMEM((blocks, band, 3 * band), jnp.bfloat16),
        pltpu.VMEM((slices, part, band), f32),
        pltpu.VMEM((n - 1, part, band), f32),
        pltpu.VMEM((slices, part, band), f32),
        pltpu.VMEM((GROUPS, slices, part, group_cols), f32),
        pltpu.VMEM((GROUPS, n - 1, part, group_cols), f32),
        pltpu.VMEM((GROUPS, slices, part, group_cols), f32),
        pltpu.VMEM((turns, GROUPS, chunks // GROUPS, band // 2, LANES), f32),
        pltpu.VMEM((turns, GROUPS, chunks // GROUPS, band // 2, LANES), f32),
        pltpu.VMEM((turns, GROUPS, chunks // GROUPS, band // 2, LANES), f32),
        pltpu.VMEM((turns, GROUPS, chunks // GROUPS, band // 2, LANES), f32),
        pltpu.VMEM((GROUPS, chunks // GROUPS, band, LANES), f32),
        pltpu.VMEM((GROUPS, chunks // GROUPS, band, LANES), f32),
        pltpu.VMEM((turns, band // 4, band), f32),
        pltpu.VMEM((turns, band // 4, band), f32),
        pltpu.VMEM((turns, band // 4, band), f32),
        pltpu.VMEM((turns, band // 4, band), f32),
        dma((turns, 4)),
        dma((chunks,)),
        dma((turns, GROUPS)),
        dma((turns, GROUPS)),
        dma((turns, GROUPS)),
        dma((turns, GROUPS)),
        dma((sweeps, blocks)),
        dma((sweeps, blocks)),
        dma((sweeps, blocks)),
        dma((4 + 4 * GROUPS,)),
    ]
    return pl.pallas_call(
        functools.partial(kernel, sizes),
        out_shape=jax.ShapeDtypeStruct((rows, cols), f32),
        in_specs=[smem, smem] + [pl.BlockSpec(memory_space=pl.ANY)] * 4,
        out_specs=vmem,
        scratch_shapes=scratch,
        compiler_params=pltpu.CompilerParams(
            collective_id=0, has_side_effects=True, vmem_limit_bytes=65_900_000
        ),
    )(sweep_start, block_len.T, flat, tfactors, panel, eigvecs)


def solution(mesh):
    in_specs = (
        P(),
        P(None, "row"),
        P("col", "row", None, None),
        P("col", "row", None, None),
        P("row", None),
        P("row", "col"),
    )
    return jax.shard_map(body, mesh=mesh, in_specs=in_specs, out_specs=P("row", "col"), check_vma=False)
```

```python
import functools

import jax
import jax.numpy as jnp
from jax import lax
from jax.experimental import pallas as pl
from jax.experimental.pallas import tpu as pltpu
from jax.sharding import PartitionSpec as P

MESH = pl.DeviceIdType.MESH
LANES = 128
GROUPS = 2


def split(value):
    high = value.astype(jnp.bfloat16)
    return high, (value - high.astype(jnp.float32)).astype(jnp.bfloat16)


def mm(left, right):
    return jnp.dot(left, right, preferred_element_type=jnp.float32)


def mm_nt(left, right):
    return lax.dot_general(left, right, (((1,), (1,)), ((), ())), preferred_element_type=jnp.float32)


def three(product, left, right):
    (lh, ll), (rh, rl) = split(left), split(right)
    return product(lh, rh) + product(lh, rl) + product(ll, rh)


def wide_left(value):
    high, low = split(value)
    return jnp.concatenate(
        [jnp.concatenate([high, high], axis=1), jnp.concatenate([low, low], axis=1)], axis=0
    )


def tall_right(value):
    return jnp.concatenate(split(value), axis=0)


def fold_halves(both):
    many = both.shape[0] // 2
    return both[:many] + both[many:]


def mm4(left, right):
    return fold_halves(mm(left, right))


def kernel(
    sizes, start_ref, len_ref, reflect_hbm, factor_hbm, panel_hbm, eig_ref, out_ref, *scratch
):
    n, nc, sweeps, owned, blocks, band, width, rows, slices = sizes
    half = band // 2
    chunks = eig_ref.shape[1] // LANES
    per_group = chunks // GROUPS
    group_cols = per_group * LANES
    slice_rows = band // slices
    first, middle_end = 2 * half, 2 * half + rows

    count = (sweeps + 1) * GROUPS
    exts, scratch = scratch[:count], scratch[count:]
    (reflect_ref, factor_ref, panel_ref, early, load_sem, packed, pt, gram_out, gram_in, gram_full, proj_out, proj_in, proj_full,
     up_out, up_in, down_out, down_in, known_up, known_down,
     head_out, head_in, tail_out, tail_in, corner_sems,
     eig_sem, up_send, up_recv, down_send, down_recv,
     right_send, left_send, piece_recv, sum_sems) = scratch

    me = lax.axis_index("row")
    z = lax.axis_index("col")

    def ext(t, g):
        return exts[t * GROUPS + g]

    barrier = pltpu.get_barrier_semaphore()
    for k in range(1, n):
        pl.semaphore_signal(barrier, inc=1, device_id={"row": lax.rem(me + k, n)}, device_id_type=MESH)
    for k in range(1, nc):
        pl.semaphore_signal(barrier, inc=1, device_id={"col": lax.rem(z + k, nc)}, device_id_type=MESH)

    block_loads = [
        pltpu.make_async_copy(reflect_hbm, reflect_ref, load_sem.at[0]),
        pltpu.make_async_copy(factor_hbm, factor_ref, load_sem.at[1]),
    ]
    panel_load = pltpu.make_async_copy(panel_hbm, panel_ref.at[half:half + rows], load_sem.at[2])
    for copy in block_loads:
        copy.start()
    loads = []
    for c in range(chunks):
        g, i = divmod(c, per_group)
        copy = pltpu.make_async_copy(
            eig_ref.at[:, c * LANES:(c + 1) * LANES],
            ext(0, g).at[i, first:middle_end],
            eig_sem.at[c],
        )
        copy.start()
        loads.append(copy)
    panel_load.start()

    flat_row = lax.broadcasted_iota(jnp.int32, (width, band), 0)
    flat_col = lax.broadcasted_iota(jnp.int32, (width, band), 1)
    right_of = flat_col > flat_row
    unit = (flat_col == flat_row).astype(jnp.float32)
    for copy in block_loads:
        copy.wait()
    for i in range(owned):
        for b in range(blocks):
            turned = jnp.transpose(factor_ref[i, b])
            turned = jnp.concatenate([turned, jnp.zeros((width, band - width), jnp.float32)], axis=1)
            packed[z * owned + i, b] = jnp.where(right_of, reflect_ref[i, b], turned)

    zeros = jnp.zeros((half, LANES), jnp.float32)
    turns = sweeps // 2 + 1

    @pl.when(me == 0)
    def _():
        panel_ref[:half] = zeros
        tail_in[...] = jnp.zeros_like(tail_in)
        for t in range(sweeps + 1):
            for g in range(GROUPS):
                for i in range(per_group):
                    ext(t, g)[i, :half] = zeros
                    if t == 0:
                        ext(t, g)[i, half:first] = zeros

    @pl.when(me == n - 1)
    def _():
        panel_ref[half + rows:] = zeros
        head_in[...] = jnp.zeros_like(head_in)
        for turn in range(turns):
            for g in range(GROUPS):
                for i in range(per_group):
                    up_in[turn, g, i] = zeros

    pl.semaphore_wait(barrier, n - 1 + nc - 1)

    def piece(s, b, to_right):
        sems = right_send if to_right else left_send
        return pltpu.make_async_remote_copy(
            packed.at[s, b], packed.at[s, b], sems.at[s, b], piece_recv.at[s, b],
            device_id={"col": z + 1 if to_right else z - 1}, device_id_type=MESH,
        )

    def send_own(i, to_right):
        for b in range(blocks):
            piece_copy = pltpu.make_async_remote_copy(
                packed.at[z * owned + i, b], packed.at[z * owned + i, b],
                (right_send if to_right else left_send).at[z * owned + i, b],
                piece_recv.at[z * owned + i, b],
                device_id={"col": z + 1 if to_right else z - 1}, device_id_type=MESH,
            )
            piece_copy.start()

    @pl.when(z == 0)
    def _():
        for i in range(owned):
            send_own(i, True)

    @pl.when(jnp.logical_and(z > 0, z < nc - 1))
    def _():
        send_own(0, True)

    @pl.when(z > 0)
    def _():
        for i in range(owned):
            send_own(i, False)

    forwards = {}
    waited_early = {}
    for s in range(sweeps):
        origin = s // owned
        for where in range(origin + 1, nc - 1):
            step = 0 if s < owned else s - 1
            forwards.setdefault(step, []).append((s, where, True))
            waited_early.setdefault(s, []).append(where)
        for where in range(1, origin):
            step = min(s, s % owned + 1 + owned * (origin - where - 1))
            forwards.setdefault(step, []).append((s, where, False))
            waited_early.setdefault(s, []).append(where)

    def gather_step(t):
        for s, where, to_right in forwards.get(t, []):
            @pl.when(z == where)
            def _():
                for b in range(blocks):
                    copy = piece(s, b, to_right)
                    copy.wait_recv()
                    copy.start()
        if t % 2 == 1:
            mine = (t + 1) // 2
            if mine < nc - 1:
                @pl.when(z == mine)
                def _():
                    for i in range(1, owned):
                        send_own(i, True)
        keep = z != t // owned
        for where in waited_early.get(t, []):
            keep = jnp.logical_and(keep, z != where)

        @pl.when(keep)
        def _():
            for b in range(blocks):
                pltpu.make_async_copy(packed.at[t, b], packed.at[t, b], piece_recv.at[t, b]).wait()

    def finish_gather():
        for s in range(sweeps):
            origin = s // owned

            @pl.when(jnp.logical_and(z >= origin, z < nc - 1))
            def _():
                for b in range(blocks):
                    piece(s, b, True).wait_send()

            @pl.when(jnp.logical_and(z <= origin, z > 0))
            def _():
                for b in range(blocks):
                    piece(s, b, False).wait_send()

    def up_copy(t, g):
        turn = (t + 1) // 2
        source = ext(0, g).at[:, first:first + half] if t == 0 else up_out.at[turn, g]
        return pltpu.make_async_remote_copy(
            source, up_in.at[turn, g],
            up_send.at[turn, g], up_recv.at[turn, g], device_id={"row": me - 1}, device_id_type=MESH,
        )

    def down_copy(t, g):
        turn = (t + 1) // 2
        return pltpu.make_async_remote_copy(
            down_out.at[turn, g], down_in.at[turn, g],
            down_send.at[turn, g], down_recv.at[turn, g], device_id={"row": me + 1}, device_id_type=MESH,
        )

    def head_copy(t):
        turn = (t + 1) // 2
        return pltpu.make_async_remote_copy(
            head_out.at[turn], head_in.at[turn], corner_sems.at[turn, 0], corner_sems.at[turn, 1],
            device_id={"row": me - 1}, device_id_type=MESH,
        )

    def tail_copy(t):
        turn = (t + 1) // 2
        return pltpu.make_async_remote_copy(
            tail_out.at[turn], tail_in.at[turn], corner_sems.at[turn, 2], corner_sems.at[turn, 3],
            device_id={"row": me + 1}, device_id_type=MESH,
        )

    def halo_start(t, g):
        @pl.when(me > 0)
        def _():
            up_copy(t, g).start()
        if t > 0:
            @pl.when(me < n - 1)
            def _():
                down_copy(t, g).start()

    def halo_take(t, g):
        turn = (t + 1) // 2
        here = ext(t, g)

        @pl.when(me < n - 1)
        def _():
            up_copy(t, g).wait_recv()

        for i in range(per_group):
            here[i, middle_end:middle_end + half] = up_in[turn, g, i]
        if t > 0:
            @pl.when(me > 0)
            def _():
                down_copy(t, g).wait_recv()
                for i in range(per_group):
                    here[i, half:first] = down_in[turn, g, i]

    def finish_halo():
        for t in [0] + list(range(1, sweeps, 2)):
            for g in range(GROUPS):
                @pl.when(me > 0)
                def _():
                    up_copy(t, g).wait_send()
                if t > 0:
                    @pl.when(me < n - 1)
                    def _():
                        down_copy(t, g).wait_send()
            if t > 0:
                if t < sweeps - 1:
                    @pl.when(me > 0)
                    def _():
                        head_copy(t).wait_send()

                @pl.when(me < n - 1)
                def _():
                    tail_copy(t).wait_send()

    def owner_only(owner, run):
        if slices == n:
            run()
        else:
            pl.when(owner < slices)(run)

    def owners_differ(refs, sem):
        def wait(many):
            view = refs.at[pl.ds(0, many)]
            pltpu.make_async_copy(view, view, sem).wait()

        if slices == n:
            wait(slices - 1)
        else:
            pl.when(me < slices)(lambda: wait(slices - 1))
            pl.when(me >= slices)(lambda: wait(slices))

    def scatter_start(out, into, base):
        for k in range(1, n):
            peer = lax.rem(me + k, n)

            def run():
                pltpu.make_async_remote_copy(
                    out.at[peer], into.at[n - k - 1], sum_sems.at[base], sum_sems.at[base + 1],
                    device_id={"row": peer}, device_id_type=MESH,
                ).start()

            owner_only(peer, run)

    def reduce_and_spread(out, into, full, base):
        def run():
            pltpu.make_async_copy(into, into, sum_sems.at[base + 1]).wait()
            total = out[me]
            for k in range(n - 1):
                total = total + into[k]
            full[me] = total
            for k in range(1, n):
                pltpu.make_async_remote_copy(
                    full.at[me], full.at[me], sum_sems.at[base + 2], sum_sems.at[base + 3],
                    device_id={"row": lax.rem(me + k, n)}, device_id_type=MESH,
                ).start()

        owner_only(me, run)

    def spread_wait(full, base):
        owners_differ(full, sum_sems.at[base + 3])

    def finish_sum(out, into, base):
        owners_differ(out, sum_sems.at[base])

        def run():
            pltpu.make_async_copy(into, into, sum_sems.at[base + 2]).wait()

        owner_only(me, run)

    for copy in loads:
        copy.wait()
    for g in range(GROUPS):
        halo_start(0, g)

    panel_load.wait()
    panel_up = pltpu.make_async_remote_copy(
        panel_ref.at[half:2 * half], panel_ref.at[half + rows:2 * half + rows],
        load_sem.at[3], load_sem.at[4], device_id={"row": me - 1}, device_id_type=MESH,
    )

    @pl.when(me > 0)
    def _():
        panel_up.start()

    transposed = jnp.transpose(panel_ref[half:half + rows])
    for b in range(blocks):
        pt[b] = wide_left(transposed[:, b * band:(b + 1) * band])
    gram = mm4(pt[0], tall_right(panel_ref[half:half + band]))
    for b in range(1, blocks):
        gram = gram + mm4(pt[b], tall_right(panel_ref[half + b * band:half + (b + 1) * band]))
    for k in range(slices):
        gram_out[k] = gram[k * slice_rows:(k + 1) * slice_rows]
    scatter_start(gram_out, gram_in, 0)

    highest = lax.Precision.HIGHEST
    row_id = lax.broadcasted_iota(jnp.int32, (band, band), 0)
    col_id = lax.broadcasted_iota(jnp.int32, (band, band), 1)
    identity = (row_id == col_id).astype(jnp.float32)
    state = {}

    def factor_start():
        spread_wait(gram_full, 0)
        total = jnp.concatenate([gram_full[k] for k in range(slices)], axis=0)
        diagonal = 0.5 * total * identity
        state["by_col"] = jnp.sum(diagonal, axis=0, keepdims=True)
        by_row = jnp.sum(diagonal, axis=1, keepdims=True)
        state["power"] = jnp.where(row_id < col_id, total, 0.0) / by_row
        state["inverse"] = identity - state["power"]
        state["reach"] = 1

    def factor_more():
        if state["reach"] * 2 < band:
            state["power"] = jnp.dot(
                state["power"], state["power"], precision=highest, preferred_element_type=jnp.float32
            )
            state["inverse"] = jnp.dot(
                state["inverse"], identity + state["power"],
                precision=highest, preferred_element_type=jnp.float32,
            )
            state["reach"] *= 2

    def offset(t):
        return start_ref[t] if 0 <= t < sweeps else 0

    def delta(t):
        return offset(t) - offset(t - 1)

    def take(ref, at, many):
        return jnp.concatenate([ref[i, pl.ds(at, many), :] for i in range(per_group)], axis=1)

    def put(ref, at, value):
        for i in range(per_group):
            ref[i, at:at + value.shape[0]] = value[:, i * LANES:(i + 1) * LANES]

    band_row = lax.broadcasted_iota(jnp.int32, (band, group_cols), 0)
    half_row = lax.broadcasted_iota(jnp.int32, (half, group_cols), 0)
    squares = {}
    corners = {}

    def prepare(t):
        gather_step(t)
        plain = []
        squares[t] = []
        for b in range(blocks):
            pack = packed[t, b]
            flat = jnp.where(right_of, pack, unit)
            flat = jnp.where(flat_col < len_ref[b, t], flat, 0.0)
            turned = jnp.where(right_of, 0.0, pack)[:, :width]
            scaled = fold_halves(mm_nt(wide_left(jnp.transpose(flat)), jnp.concatenate(split(turned), axis=1)))
            square = mm4(wide_left(scaled), tall_right(flat))
            plain.append(square)
            squares[t].append(wide_left(square))
            if t == sweeps - 1:
                if b == 0:
                    @pl.when(me < n - 1)
                    def _():
                        panel_up.wait_recv()
                side = jnp.transpose(panel_ref[pl.ds(half + b * band + start_ref[t], band), :])
                early[b] = wide_left(side - mm4(wide_left(side), tall_right(square)))
        if t % 2 == 1:
            turn = (t + 1) // 2
            quarter = half // 2

            def fold(corner):
                return jnp.concatenate([corner[:quarter], corner[quarter:]], axis=1)

            if t < sweeps - 1:
                head_out[turn] = fold((identity - plain[0])[:half, :half])

                @pl.when(me > 0)
                def _():
                    head_copy(t).start()
            tail_out[turn] = fold((identity - plain[-1])[half:, half:])

            @pl.when(me < n - 1)
            def _():
                tail_copy(t).start()

    def corner_take(t):
        turn = (t + 1) // 2

        def unfold(both):
            return wide_left(jnp.concatenate([both[:, :half], both[:, half:]], axis=0))

        if t < sweeps - 1:
            @pl.when(me < n - 1)
            def _():
                head_copy(t).wait_recv()
            corners[t, 0] = unfold(head_in[turn])

        @pl.when(me > 0)
        def _():
            tail_copy(t).wait_recv()
        corners[t, 1] = unfold(tail_in[turn])

    def part(wide, at):
        return jnp.concatenate([wide[at:at + half], wide[band + at:band + at + half]], axis=0)

    def send_ahead(t, g):
        turn = (t + 1) // 2
        here = ext(t, g)
        move = delta(t)
        down_by, up_by = jnp.maximum(move, 0), jnp.maximum(-move, 0)
        top = take(here, first, half)
        if t < sweeps - 1:
            window = take(here, first + move, band)
            window = jnp.where(band_row + move >= 0, window, 0.0)
            put(known_up.at[g], half, window[:half] - mm4(part(squares[t][0], 0), tall_right(window)))
            top = jnp.where(half_row < down_by, top, take(known_up.at[g], half - down_by, half))
        put(up_out.at[turn, g], 0, top)
        window = take(here, first + (blocks - 1) * band + move, band)
        window = jnp.where(band_row + move < band, window, 0.0)
        put(known_down.at[g], 0, window[half:] - mm4(part(squares[t][-1], half), tall_right(window)))
        low = jnp.where(
            half_row >= half - up_by, take(here, middle_end - half, half), take(known_down.at[g], up_by, half)
        )
        put(down_out.at[turn, g], 0, low)
        halo_start(t, g)

    def sweep(t, g):
        here, after = ext(t, g), ext(t + 1, g)
        move = delta(t)
        total = None
        for b in range(blocks):
            window = take(here, first + b * band + move, band)
            tall = tall_right(window)
            if t == sweeps - 1:
                term = mm4(early[b], tall)
                total = term if total is None else total + term
            put(after, first + b * band, window - mm4(squares[t][b], tall))
        if t % 2 == 1:
            shift = jnp.where(me == 0, move, jnp.minimum(move, 0))
            lead = jnp.where(half_row >= half - move, take(here, first + move - half, half), 0.0)
            put(after, half, take(here, half + shift, half) + mm4(corners[t, 1], tall_right(lead)))
            if t < sweeps - 1:
                rest = jnp.where(half_row < -move, take(here, middle_end + move, half), 0.0)
                put(
                    after, middle_end,
                    take(here, middle_end + jnp.maximum(move, 0), half) + mm4(corners[t, 0], tall_right(rest)),
                )
        else:
            @pl.when(me == 0)
            def _():
                put(after, half, take(here, half + move, half))
        if t == sweeps - 1:
            for k in range(slices):
                proj_out[g, k] = total[k * slice_rows:(k + 1) * slice_rows]

            @pl.when(me == 0)
            def _():
                side = jnp.transpose(panel_ref[pl.ds(start_ref[t], half), :])
                more = three(mm, side, take(here, half + move, half))
                for k in range(slices):
                    proj_out[g, k] = proj_out[g, k] + more[k * slice_rows:(k + 1) * slice_rows]

            scatter_start(proj_out.at[g], proj_in.at[g], 4 + 4 * g)

    prepare(0)
    for g in range(GROUPS):
        halo_take(0, g)
        sweep(0, g)
    prepare(1)
    for g in range(GROUPS):
        send_ahead(1, g)
    prepare(2)
    for t in range(1, sweeps, 2):
        if t + 2 < sweeps:
            prepare(t + 2)
        corner_take(t)
        for g in range(GROUPS):
            halo_take(t, g)
            sweep(t, g)
            if t + 1 < sweeps:
                sweep(t + 1, g)
                send_ahead(t + 2, g)
        if t == 1:
            reduce_and_spread(gram_out, gram_in, gram_full, 0)
        if t == 3:
            factor_start()
        if 3 <= t < sweeps - 1:
            for _ in range(4):
                factor_more()
        if t + 3 < sweeps:
            prepare(t + 3)

    for g in range(GROUPS):
        columns = slice(g * group_cols, (g + 1) * group_cols)
        here = ext(sweeps, g)
        for b in range(blocks):
            out_ref[b * band:(b + 1) * band, columns] = take(here, first + b * band + delta(sweeps), band)
        reduce_and_spread(proj_out.at[g], proj_in.at[g], proj_full.at[g], 4 + 4 * g)
    while state["reach"] * 2 < band:
        factor_more()

    factor = wide_left(state["inverse"] / state["by_col"])
    for g in range(GROUPS):
        columns = slice(g * group_cols, (g + 1) * group_cols)
        spread_wait(proj_full.at[g], 4 + 4 * g)
        projection = jnp.concatenate([proj_full[g, k] for k in range(slices)], axis=0)
        inner = tall_right(mm4(factor, tall_right(projection)))
        for b in range(blocks):
            span = slice(b * band, (b + 1) * band)
            out_ref[span, columns] = out_ref[span, columns] - mm4(wide_left(panel_ref[half + b * band:half + (b + 1) * band]), inner)

    @pl.when(me > 0)
    def _():
        panel_up.wait_send()

    finish_gather()
    finish_halo()
    finish_sum(gram_out, gram_in, 0)
    for g in range(GROUPS):
        finish_sum(proj_out.at[g], proj_in.at[g], 4 + 4 * g)


def body(sweep_start, block_len, reflectors, tfactors, panel, eigvecs):
    rows, cols = eigvecs.shape
    owned, blocks, band, width = reflectors.shape
    flat = jnp.swapaxes(reflectors, 2, 3)
    n, nc = lax.axis_size("row"), lax.axis_size("col")
    sweeps = owned * nc
    slices = min(n, band // 8)
    part = band // slices
    chunks = cols // LANES
    group_cols = cols // GROUPS
    turns = sweeps // 2 + 1
    sizes = (n, nc, sweeps, owned, blocks, band, width, rows, slices)
    vmem = pl.BlockSpec(memory_space=pltpu.VMEM)
    smem = pl.BlockSpec(memory_space=pltpu.SMEM)
    f32 = jnp.float32
    dma = pltpu.SemaphoreType.DMA
    scratch = [
        pltpu.VMEM((chunks // GROUPS, rows + 4 * (band // 2), LANES), f32)
        for _ in range((sweeps + 1) * GROUPS)
    ] + [
        pltpu.VMEM((owned, blocks, width, band), f32),
        pltpu.VMEM((owned, blocks, width, width), f32),
        pltpu.VMEM((rows + 2 * (band // 2), band), f32),
        pltpu.VMEM((blocks, 2 * band, 2 * band), jnp.bfloat16),
        dma((5,)),
        pltpu.VMEM((sweeps, blocks, width, 2 * width), f32),
        pltpu.VMEM((blocks, 2 * band, 2 * band), jnp.bfloat16),
        pltpu.VMEM((slices, part, band), f32),
        pltpu.VMEM((n - 1, part, band), f32),
        pltpu.VMEM((slices, part, band), f32),
        pltpu.VMEM((GROUPS, slices, part, group_cols), f32),
        pltpu.VMEM((GROUPS, n - 1, part, group_cols), f32),
        pltpu.VMEM((GROUPS, slices, part, group_cols), f32),
        pltpu.VMEM((turns, GROUPS, chunks // GROUPS, band // 2, LANES), f32),
        pltpu.VMEM((turns, GROUPS, chunks // GROUPS, band // 2, LANES), f32),
        pltpu.VMEM((turns, GROUPS, chunks // GROUPS, band // 2, LANES), f32),
        pltpu.VMEM((turns, GROUPS, chunks // GROUPS, band // 2, LANES), f32),
        pltpu.VMEM((GROUPS, chunks // GROUPS, band, LANES), f32),
        pltpu.VMEM((GROUPS, chunks // GROUPS, band, LANES), f32),
        pltpu.VMEM((turns, band // 4, band), f32),
        pltpu.VMEM((turns, band // 4, band), f32),
        pltpu.VMEM((turns, band // 4, band), f32),
        pltpu.VMEM((turns, band // 4, band), f32),
        dma((turns, 4)),
        dma((chunks,)),
        dma((turns, GROUPS)),
        dma((turns, GROUPS)),
        dma((turns, GROUPS)),
        dma((turns, GROUPS)),
        dma((sweeps, blocks)),
        dma((sweeps, blocks)),
        dma((sweeps, blocks)),
        dma((4 + 4 * GROUPS,)),
    ]
    return pl.pallas_call(
        functools.partial(kernel, sizes),
        out_shape=jax.ShapeDtypeStruct((rows, cols), f32),
        in_specs=[smem, smem] + [pl.BlockSpec(memory_space=pl.ANY)] * 4,
        out_specs=vmem,
        scratch_shapes=scratch,
        compiler_params=pltpu.CompilerParams(
            collective_id=0, has_side_effects=True, vmem_limit_bytes=65_900_000
        ),
    )(sweep_start, block_len.T, flat, tfactors, panel, eigvecs)


def solution(mesh):
    in_specs = (
        P(),
        P(None, "row"),
        P("col", "row", None, None),
        P("col", "row", None, None),
        P("row", None),
        P("row", "col"),
    )
    return jax.shard_map(body, mesh=mesh, in_specs=in_specs, out_specs=P("row", "col"), check_vma=False)
```

```python
import functools

import jax
import jax.numpy as jnp
from jax import lax
from jax.experimental import pallas as pl
from jax.experimental.pallas import tpu as pltpu
from jax.sharding import PartitionSpec as P

MESH = pl.DeviceIdType.MESH
LANES = 128
GROUPS = 2


def split(value):
    high = value.astype(jnp.bfloat16)
    return high, (value - high.astype(jnp.float32)).astype(jnp.bfloat16)


def mm(left, right):
    return jnp.dot(left, right, preferred_element_type=jnp.float32)


def mm_nt(left, right):
    return lax.dot_general(left, right, (((1,), (1,)), ((), ())), preferred_element_type=jnp.float32)


def three(product, left, right):
    (lh, ll), (rh, rl) = split(left), split(right)
    return product(lh, rh) + product(lh, rl) + product(ll, rh)


def wide_left(value):
    high, low = split(value)
    return jnp.concatenate(
        [jnp.concatenate([high, high], axis=1), jnp.concatenate([low, low], axis=1)], axis=0
    )


def tall_right(value):
    return jnp.concatenate(split(value), axis=0)


def fold_halves(both):
    many = both.shape[0] // 2
    return both[:many] + both[many:]


def mm4(left, right):
    return fold_halves(mm(left, right))


def kernel(
    sizes, start_ref, len_ref, reflect_hbm, factor_hbm, panel_hbm, eig_ref, out_ref, *scratch
):
    n, nc, sweeps, owned, blocks, band, width, rows, slices = sizes
    half = band // 2
    chunks = eig_ref.shape[1] // LANES
    per_group = chunks // GROUPS
    group_cols = per_group * LANES
    slice_rows = band // slices
    first, middle_end = 2 * half, 2 * half + rows

    count = (sweeps + 1) * GROUPS
    exts, scratch = scratch[:count], scratch[count:]
    (reflect_ref, factor_ref, panel_ref, early, load_sem, packed, pt, gram_out, gram_in, gram_full, proj_out, proj_in, proj_full,
     up_out, up_in, down_out, down_in, known_up, known_down,
     head_out, head_in, tail_out, tail_in, corner_sems, weights, weight_sems,
     eig_sem, up_send, up_recv, down_send, down_recv,
     right_send, left_send, piece_recv, sum_sems) = scratch

    me = lax.axis_index("row")
    z = lax.axis_index("col")

    def ext(t, g):
        return exts[t * GROUPS + g]

    barrier = pltpu.get_barrier_semaphore()
    for k in range(1, n):
        pl.semaphore_signal(barrier, inc=1, device_id={"row": lax.rem(me + k, n)}, device_id_type=MESH)
    for k in range(1, nc):
        pl.semaphore_signal(barrier, inc=1, device_id={"col": lax.rem(z + k, nc)}, device_id_type=MESH)

    block_loads = [
        pltpu.make_async_copy(reflect_hbm, reflect_ref, load_sem.at[0]),
        pltpu.make_async_copy(factor_hbm, factor_ref, load_sem.at[1]),
    ]
    panel_load = pltpu.make_async_copy(panel_hbm, panel_ref.at[half:half + rows], load_sem.at[2])
    for copy in block_loads:
        copy.start()
    loads = []
    for c in range(chunks):
        g, i = divmod(c, per_group)
        copy = pltpu.make_async_copy(
            eig_ref.at[:, c * LANES:(c + 1) * LANES],
            ext(0, g).at[i, first:middle_end],
            eig_sem.at[c],
        )
        copy.start()
        loads.append(copy)
    panel_load.start()

    flat_row = lax.broadcasted_iota(jnp.int32, (width, band), 0)
    flat_col = lax.broadcasted_iota(jnp.int32, (width, band), 1)
    right_of = flat_col > flat_row
    unit = (flat_col == flat_row).astype(jnp.float32)
    for copy in block_loads:
        copy.wait()
    for i in range(owned):
        for b in range(blocks):
            turned = jnp.transpose(factor_ref[i, b])
            turned = jnp.concatenate([turned, jnp.zeros((width, band - width), jnp.float32)], axis=1)
            packed[z * owned + i, b] = jnp.where(right_of, reflect_ref[i, b], turned)

    zeros = jnp.zeros((half, LANES), jnp.float32)
    turns = sweeps // 2 + 1

    @pl.when(me == 0)
    def _():
        panel_ref[:half] = zeros
        weights[:half] = zeros
        tail_in[...] = jnp.zeros_like(tail_in)
        for t in range(sweeps + 1):
            for g in range(GROUPS):
                for i in range(per_group):
                    ext(t, g)[i, :half] = zeros
                    if t == 0:
                        ext(t, g)[i, half:first] = zeros

    @pl.when(me == n - 1)
    def _():
        panel_ref[half + rows:] = zeros
        weights[middle_end:middle_end + half] = zeros
        head_in[...] = jnp.zeros_like(head_in)
        for turn in range(turns):
            for g in range(GROUPS):
                for i in range(per_group):
                    up_in[turn, g, i] = zeros

    pl.semaphore_wait(barrier, n - 1 + nc - 1)

    def piece(s, b, to_right):
        sems = right_send if to_right else left_send
        return pltpu.make_async_remote_copy(
            packed.at[s, b], packed.at[s, b], sems.at[s, b], piece_recv.at[s, b],
            device_id={"col": z + 1 if to_right else z - 1}, device_id_type=MESH,
        )

    def send_own(i, to_right):
        for b in range(blocks):
            piece_copy = pltpu.make_async_remote_copy(
                packed.at[z * owned + i, b], packed.at[z * owned + i, b],
                (right_send if to_right else left_send).at[z * owned + i, b],
                piece_recv.at[z * owned + i, b],
                device_id={"col": z + 1 if to_right else z - 1}, device_id_type=MESH,
            )
            piece_copy.start()

    @pl.when(z == 0)
    def _():
        for i in range(owned):
            send_own(i, True)

    @pl.when(jnp.logical_and(z > 0, z < nc - 1))
    def _():
        send_own(0, True)

    @pl.when(jnp.logical_and(z >= nc - 2, z < nc - 1))
    def _():
        for i in range(1, owned):
            send_own(i, True)

    @pl.when(z > 0)
    def _():
        for i in range(owned):
            send_own(i, False)

    forwards = {}
    waited_early = {}
    for s in range(sweeps):
        origin = s // owned
        for where in range(origin + 1, nc - 1):
            step = 0 if s < owned else s - 1
            forwards.setdefault(step, []).append((s, where, True))
            waited_early.setdefault(s, []).append(where)
        for where in range(1, origin):
            step = min(s, s % owned + 1 + owned * (origin - where - 1))
            forwards.setdefault(step, []).append((s, where, False))
            waited_early.setdefault(s, []).append(where)

    def gather_step(t):
        for s, where, to_right in forwards.get(t, []):
            @pl.when(z == where)
            def _():
                for b in range(blocks):
                    copy = piece(s, b, to_right)
                    copy.wait_recv()
                    copy.start()
        if t % 2 == 1:
            mine = (t + 1) // 2
            if mine < nc - 2:
                @pl.when(z == mine)
                def _():
                    for i in range(1, owned):
                        send_own(i, True)
        keep = z != t // owned
        for where in waited_early.get(t, []):
            keep = jnp.logical_and(keep, z != where)

        @pl.when(keep)
        def _():
            for b in range(blocks):
                pltpu.make_async_copy(packed.at[t, b], packed.at[t, b], piece_recv.at[t, b]).wait()

    def finish_gather():
        for s in range(sweeps):
            origin = s // owned

            @pl.when(jnp.logical_and(z >= origin, z < nc - 1))
            def _():
                for b in range(blocks):
                    piece(s, b, True).wait_send()

            @pl.when(jnp.logical_and(z <= origin, z > 0))
            def _():
                for b in range(blocks):
                    piece(s, b, False).wait_send()

    def up_copy(t, g):
        turn = (t + 1) // 2
        source = ext(0, g).at[:, first:first + half] if t == 0 else up_out.at[turn, g]
        return pltpu.make_async_remote_copy(
            source, up_in.at[turn, g],
            up_send.at[turn, g], up_recv.at[turn, g], device_id={"row": me - 1}, device_id_type=MESH,
        )

    def down_copy(t, g):
        turn = (t + 1) // 2
        return pltpu.make_async_remote_copy(
            down_out.at[turn, g], down_in.at[turn, g],
            down_send.at[turn, g], down_recv.at[turn, g], device_id={"row": me + 1}, device_id_type=MESH,
        )

    def head_copy(t):
        turn = (t + 1) // 2
        return pltpu.make_async_remote_copy(
            head_out.at[turn], head_in.at[turn], corner_sems.at[turn, 0], corner_sems.at[turn, 1],
            device_id={"row": me - 1}, device_id_type=MESH,
        )

    def tail_copy(t):
        turn = (t + 1) // 2
        return pltpu.make_async_remote_copy(
            tail_out.at[turn], tail_in.at[turn], corner_sems.at[turn, 2], corner_sems.at[turn, 3],
            device_id={"row": me + 1}, device_id_type=MESH,
        )

    def halo_start(t, g):
        @pl.when(me > 0)
        def _():
            up_copy(t, g).start()
        if t > 0:
            @pl.when(me < n - 1)
            def _():
                down_copy(t, g).start()

    def halo_take(t, g):
        turn = (t + 1) // 2
        here = ext(t, g)

        @pl.when(me < n - 1)
        def _():
            up_copy(t, g).wait_recv()

        for i in range(per_group):
            here[i, middle_end:middle_end + half] = up_in[turn, g, i]
        if t > 0:
            @pl.when(me > 0)
            def _():
                down_copy(t, g).wait_recv()
                for i in range(per_group):
                    here[i, half:first] = down_in[turn, g, i]

    def finish_halo():
        for t in [0] + list(range(1, sweeps, 2)):
            for g in range(GROUPS):
                @pl.when(me > 0)
                def _():
                    up_copy(t, g).wait_send()
                if t > 0:
                    @pl.when(me < n - 1)
                    def _():
                        down_copy(t, g).wait_send()
            if t > 0:
                if t < sweeps - 1:
                    @pl.when(me > 0)
                    def _():
                        head_copy(t).wait_send()

                @pl.when(me < n - 1)
                def _():
                    tail_copy(t).wait_send()

    def owner_only(owner, run):
        if slices == n:
            run()
        else:
            pl.when(owner < slices)(run)

    def owners_differ(refs, sem):
        def wait(many):
            view = refs.at[pl.ds(0, many)]
            pltpu.make_async_copy(view, view, sem).wait()

        if slices == n:
            wait(slices - 1)
        else:
            pl.when(me < slices)(lambda: wait(slices - 1))
            pl.when(me >= slices)(lambda: wait(slices))

    def scatter_start(out, into, base):
        for k in range(1, n):
            peer = lax.rem(me + k, n)

            def run():
                pltpu.make_async_remote_copy(
                    out.at[peer], into.at[n - k - 1], sum_sems.at[base], sum_sems.at[base + 1],
                    device_id={"row": peer}, device_id_type=MESH,
                ).start()

            owner_only(peer, run)

    def reduce_and_spread(out, into, full, base):
        def run():
            pltpu.make_async_copy(into, into, sum_sems.at[base + 1]).wait()
            total = out[me]
            for k in range(n - 1):
                total = total + into[k]
            full[me] = total
            for k in range(1, n):
                pltpu.make_async_remote_copy(
                    full.at[me], full.at[me], sum_sems.at[base + 2], sum_sems.at[base + 3],
                    device_id={"row": lax.rem(me + k, n)}, device_id_type=MESH,
                ).start()

        owner_only(me, run)

    def spread_wait(full, base):
        owners_differ(full, sum_sems.at[base + 3])

    def finish_sum(out, into, base):
        owners_differ(out, sum_sems.at[base])

        def run():
            pltpu.make_async_copy(into, into, sum_sems.at[base + 2]).wait()

        owner_only(me, run)

    for copy in loads:
        copy.wait()
    for g in range(GROUPS):
        halo_start(0, g)

    panel_load.wait()
    panel_up = pltpu.make_async_remote_copy(
        panel_ref.at[half:2 * half], panel_ref.at[half + rows:2 * half + rows],
        load_sem.at[3], load_sem.at[4], device_id={"row": me - 1}, device_id_type=MESH,
    )

    @pl.when(me > 0)
    def _():
        panel_up.start()

    transposed = jnp.transpose(panel_ref[half:half + rows])
    for b in range(blocks):
        pt[b] = wide_left(transposed[:, b * band:(b + 1) * band])
    gram = mm4(pt[0], tall_right(panel_ref[half:half + band]))
    for b in range(1, blocks):
        gram = gram + mm4(pt[b], tall_right(panel_ref[half + b * band:half + (b + 1) * band]))
    for k in range(slices):
        gram_out[k] = gram[k * slice_rows:(k + 1) * slice_rows]
    scatter_start(gram_out, gram_in, 0)

    highest = lax.Precision.HIGHEST
    row_id = lax.broadcasted_iota(jnp.int32, (band, band), 0)
    col_id = lax.broadcasted_iota(jnp.int32, (band, band), 1)
    identity = (row_id == col_id).astype(jnp.float32)
    state = {}

    def factor_start():
        spread_wait(gram_full, 0)
        total = jnp.concatenate([gram_full[k] for k in range(slices)], axis=0)
        diagonal = 0.5 * total * identity
        state["by_col"] = jnp.sum(diagonal, axis=0, keepdims=True)
        by_row = jnp.sum(diagonal, axis=1, keepdims=True)
        state["power"] = jnp.where(row_id < col_id, total, 0.0) / by_row
        state["inverse"] = identity - state["power"]
        state["reach"] = 1

    def factor_more():
        if state["reach"] * 2 < band:
            state["power"] = jnp.dot(
                state["power"], state["power"], precision=highest, preferred_element_type=jnp.float32
            )
            state["inverse"] = jnp.dot(
                state["inverse"], identity + state["power"],
                precision=highest, preferred_element_type=jnp.float32,
            )
            state["reach"] *= 2

    def offset(t):
        return start_ref[t] if 0 <= t < sweeps else 0

    def delta(t):
        return offset(t) - offset(t - 1)

    def take(ref, at, many):
        return jnp.concatenate([ref[i, pl.ds(at, many), :] for i in range(per_group)], axis=1)

    def put(ref, at, value):
        for i in range(per_group):
            ref[i, at:at + value.shape[0]] = value[:, i * LANES:(i + 1) * LANES]

    band_row = lax.broadcasted_iota(jnp.int32, (band, group_cols), 0)
    half_row = lax.broadcasted_iota(jnp.int32, (half, group_cols), 0)
    squares = {}
    corners = {}

    weight_up = pltpu.make_async_remote_copy(
        weights.at[first:first + half], weights.at[middle_end:middle_end + half],
        weight_sems.at[0], weight_sems.at[1], device_id={"row": me - 1}, device_id_type=MESH,
    )
    weight_down = pltpu.make_async_remote_copy(
        weights.at[middle_end - half:middle_end], weights.at[half:first],
        weight_sems.at[2], weight_sems.at[3], device_id={"row": me + 1}, device_id_type=MESH,
    )

    def weights_take():
        @pl.when(me < n - 1)
        def _():
            weight_up.wait_recv()

        @pl.when(me > 0)
        def _():
            weight_down.wait_recv()

        for b in range(blocks):
            early[b] = wide_left(
                jnp.transpose(weights[pl.ds(first + b * band - delta(sweeps - 1), band), :])
            )

    def project(g):
        here = ext(sweeps - 1, g)
        total = mm4(early[0], tall_right(take(here, first, band)))
        for b in range(1, blocks):
            total = total + mm4(early[b], tall_right(take(here, first + b * band, band)))
        for k in range(slices):
            proj_out[g, k] = total[k * slice_rows:(k + 1) * slice_rows]

        @pl.when(me == 0)
        def _():
            side = jnp.transpose(weights[pl.ds(first - half - delta(sweeps - 1), half), :])
            more = three(mm, side, take(here, half, half))
            for k in range(slices):
                proj_out[g, k] = proj_out[g, k] + more[k * slice_rows:(k + 1) * slice_rows]

        scatter_start(proj_out.at[g], proj_in.at[g], 4 + 4 * g)

    def prepare(t):
        gather_step(t)
        plain = []
        squares[t] = []
        for b in range(blocks):
            pack = packed[t, b]
            flat = jnp.where(right_of, pack, unit)
            flat = jnp.where(flat_col < len_ref[b, t], flat, 0.0)
            turned = jnp.where(right_of, 0.0, pack)[:, :width]
            scaled = fold_halves(mm_nt(wide_left(jnp.transpose(flat)), jnp.concatenate(split(turned), axis=1)))
            square = mm4(wide_left(scaled), tall_right(flat))
            plain.append(square)
            squares[t].append(wide_left(square))
            if t == sweeps - 1:
                if b == 0:
                    @pl.when(me < n - 1)
                    def _():
                        panel_up.wait_recv()
                side = panel_ref[pl.ds(half + b * band + start_ref[t], band), :]
                weights[first + b * band:first + (b + 1) * band] = side - mm4(
                    wide_left(jnp.transpose(square)), tall_right(side)
                )
        if t == sweeps - 1:
            @pl.when(me == 0)
            def _():
                weights[half:first] = panel_ref[pl.ds(start_ref[t], half), :]

            @pl.when(me > 0)
            def _():
                weight_up.start()

            @pl.when(me < n - 1)
            def _():
                weight_down.start()
        if t % 2 == 1:
            turn = (t + 1) // 2
            quarter = half // 2

            def fold(corner):
                return jnp.concatenate([corner[:quarter], corner[quarter:]], axis=1)

            if t < sweeps - 1:
                head_out[turn] = fold((identity - plain[0])[:half, :half])

                @pl.when(me > 0)
                def _():
                    head_copy(t).start()
            tail_out[turn] = fold((identity - plain[-1])[half:, half:])

            @pl.when(me < n - 1)
            def _():
                tail_copy(t).start()

    def corner_take(t):
        turn = (t + 1) // 2

        def unfold(both):
            return wide_left(jnp.concatenate([both[:, :half], both[:, half:]], axis=0))

        if t < sweeps - 1:
            @pl.when(me < n - 1)
            def _():
                head_copy(t).wait_recv()
            corners[t, 0] = unfold(head_in[turn])

        @pl.when(me > 0)
        def _():
            tail_copy(t).wait_recv()
        corners[t, 1] = unfold(tail_in[turn])

    def part(wide, at):
        return jnp.concatenate([wide[at:at + half], wide[band + at:band + at + half]], axis=0)

    def send_ahead(t, g):
        turn = (t + 1) // 2
        here = ext(t, g)
        move = delta(t)
        down_by, up_by = jnp.maximum(move, 0), jnp.maximum(-move, 0)
        top = take(here, first, half)
        if t < sweeps - 1:
            window = take(here, first + move, band)
            window = jnp.where(band_row + move >= 0, window, 0.0)
            put(known_up.at[g], half, window[:half] - mm4(part(squares[t][0], 0), tall_right(window)))
            top = jnp.where(half_row < down_by, top, take(known_up.at[g], half - down_by, half))
        put(up_out.at[turn, g], 0, top)
        window = take(here, first + (blocks - 1) * band + move, band)
        window = jnp.where(band_row + move < band, window, 0.0)
        put(known_down.at[g], 0, window[half:] - mm4(part(squares[t][-1], half), tall_right(window)))
        low = jnp.where(
            half_row >= half - up_by, take(here, middle_end - half, half), take(known_down.at[g], up_by, half)
        )
        put(down_out.at[turn, g], 0, low)
        halo_start(t, g)

    def sweep(t, g):
        here, after = ext(t, g), ext(t + 1, g)
        move = delta(t)
        for b in range(blocks):
            window = take(here, first + b * band + move, band)
            put(after, first + b * band, window - mm4(squares[t][b], tall_right(window)))
        if t % 2 == 1:
            shift = jnp.where(me == 0, move, jnp.minimum(move, 0))
            lead = jnp.where(half_row >= half - move, take(here, first + move - half, half), 0.0)
            put(after, half, take(here, half + shift, half) + mm4(corners[t, 1], tall_right(lead)))
            if t < sweeps - 1:
                rest = jnp.where(half_row < -move, take(here, middle_end + move, half), 0.0)
                put(
                    after, middle_end,
                    take(here, middle_end + jnp.maximum(move, 0), half) + mm4(corners[t, 0], tall_right(rest)),
                )
        else:
            @pl.when(me == 0)
            def _():
                put(after, half, take(here, half + move, half))

    prepare(0)
    for g in range(GROUPS):
        halo_take(0, g)
        sweep(0, g)
    prepare(1)
    for g in range(GROUPS):
        send_ahead(1, g)
    prepare(2)
    for t in range(1, sweeps, 2):
        merged = t + 1 < sweeps
        if merged:
            prepare(t + 2)
        corner_take(t)
        for g in range(GROUPS):
            halo_take(t, g)
            sweep(t, g)
            if t + 1 < sweeps:
                sweep(t + 1, g)
                if merged:
                    send_ahead(t + 2, g)
            else:
                reduce_and_spread(proj_out.at[g], proj_in.at[g], proj_full.at[g], 4 + 4 * g)
        if t + 1 < sweeps:
            if not merged:
                prepare(t + 2)
                for g in range(GROUPS):
                    send_ahead(t + 2, g)
            if t + 3 == sweeps:
                weights_take()
                for g in range(GROUPS):
                    project(g)
        if t == 1:
            reduce_and_spread(gram_out, gram_in, gram_full, 0)
        if t == 3:
            factor_start()
        if 3 <= t < sweeps - 1:
            for _ in range(4):
                factor_more()
        if t + 3 < sweeps:
            prepare(t + 3)

    for g in range(GROUPS):
        columns = slice(g * group_cols, (g + 1) * group_cols)
        here = ext(sweeps, g)
        for b in range(blocks):
            out_ref[b * band:(b + 1) * band, columns] = take(here, first + b * band + delta(sweeps), band)
    while state["reach"] * 2 < band:
        factor_more()

    factor = wide_left(state["inverse"] / state["by_col"])
    for g in range(GROUPS):
        columns = slice(g * group_cols, (g + 1) * group_cols)
        spread_wait(proj_full.at[g], 4 + 4 * g)
        projection = jnp.concatenate([proj_full[g, k] for k in range(slices)], axis=0)
        inner = tall_right(mm4(factor, tall_right(projection)))
        for b in range(blocks):
            span = slice(b * band, (b + 1) * band)
            out_ref[span, columns] = out_ref[span, columns] - mm4(wide_left(panel_ref[half + b * band:half + (b + 1) * band]), inner)

    @pl.when(me > 0)
    def _():
        panel_up.wait_send()
        weight_up.wait_send()

    @pl.when(me < n - 1)
    def _():
        weight_down.wait_send()

    finish_gather()
    finish_halo()
    finish_sum(gram_out, gram_in, 0)
    for g in range(GROUPS):
        finish_sum(proj_out.at[g], proj_in.at[g], 4 + 4 * g)


def body(sweep_start, block_len, reflectors, tfactors, panel, eigvecs):
    rows, cols = eigvecs.shape
    owned, blocks, band, width = reflectors.shape
    flat = jnp.swapaxes(reflectors, 2, 3)
    n, nc = lax.axis_size("row"), lax.axis_size("col")
    sweeps = owned * nc
    slices = min(n, band // 8)
    part = band // slices
    chunks = cols // LANES
    group_cols = cols // GROUPS
    turns = sweeps // 2 + 1
    sizes = (n, nc, sweeps, owned, blocks, band, width, rows, slices)
    vmem = pl.BlockSpec(memory_space=pltpu.VMEM)
    smem = pl.BlockSpec(memory_space=pltpu.SMEM)
    f32 = jnp.float32
    dma = pltpu.SemaphoreType.DMA
    scratch = [
        pltpu.VMEM((chunks // GROUPS, rows + 4 * (band // 2), LANES), f32)
        for _ in range((sweeps + 1) * GROUPS)
    ] + [
        pltpu.VMEM((owned, blocks, width, band), f32),
        pltpu.VMEM((owned, blocks, width, width), f32),
        pltpu.VMEM((rows + 2 * (band // 2), band), f32),
        pltpu.VMEM((blocks, 2 * band, 2 * band), jnp.bfloat16),
        dma((5,)),
        pltpu.VMEM((sweeps, blocks, width, 2 * width), f32),
        pltpu.VMEM((blocks, 2 * band, 2 * band), jnp.bfloat16),
        pltpu.VMEM((slices, part, band), f32),
        pltpu.VMEM((n - 1, part, band), f32),
        pltpu.VMEM((slices, part, band), f32),
        pltpu.VMEM((GROUPS, slices, part, group_cols), f32),
        pltpu.VMEM((GROUPS, n - 1, part, group_cols), f32),
        pltpu.VMEM((GROUPS, slices, part, group_cols), f32),
        pltpu.VMEM((turns, GROUPS, chunks // GROUPS, band // 2, LANES), f32),
        pltpu.VMEM((turns, GROUPS, chunks // GROUPS, band // 2, LANES), f32),
        pltpu.VMEM((turns, GROUPS, chunks // GROUPS, band // 2, LANES), f32),
        pltpu.VMEM((turns, GROUPS, chunks // GROUPS, band // 2, LANES), f32),
        pltpu.VMEM((GROUPS, chunks // GROUPS, band, LANES), f32),
        pltpu.VMEM((GROUPS, chunks // GROUPS, band, LANES), f32),
        pltpu.VMEM((turns, band // 4, band), f32),
        pltpu.VMEM((turns, band // 4, band), f32),
        pltpu.VMEM((turns, band // 4, band), f32),
        pltpu.VMEM((turns, band // 4, band), f32),
        dma((turns, 4)),
        pltpu.VMEM((rows + 4 * (band // 2), band), f32),
        dma((4,)),
        dma((chunks,)),
        dma((turns, GROUPS)),
        dma((turns, GROUPS)),
        dma((turns, GROUPS)),
        dma((turns, GROUPS)),
        dma((sweeps, blocks)),
        dma((sweeps, blocks)),
        dma((sweeps, blocks)),
        dma((4 + 4 * GROUPS,)),
    ]
    return pl.pallas_call(
        functools.partial(kernel, sizes),
        out_shape=jax.ShapeDtypeStruct((rows, cols), f32),
        in_specs=[smem, smem] + [pl.BlockSpec(memory_space=pl.ANY)] * 4,
        out_specs=vmem,
        scratch_shapes=scratch,
        compiler_params=pltpu.CompilerParams(
            collective_id=0, has_side_effects=True, vmem_limit_bytes=65_900_000
        ),
    )(sweep_start, block_len.T, flat, tfactors, panel, eigvecs)


def solution(mesh):
    in_specs = (
        P(),
        P(None, "row"),
        P("col", "row", None, None),
        P("col", "row", None, None),
        P("row", None),
        P("row", "col"),
    )
    return jax.shard_map(body, mesh=mesh, in_specs=in_specs, out_specs=P("row", "col"), check_vma=False)
```

```python
import functools

import jax
import jax.numpy as jnp
from jax import lax
from jax.experimental import pallas as pl
from jax.experimental.pallas import tpu as pltpu
from jax.sharding import PartitionSpec as P

MESH = pl.DeviceIdType.MESH
LANES = 128
GROUPS = 2


def split(value):
    high = value.astype(jnp.bfloat16)
    return high, (value - high.astype(jnp.float32)).astype(jnp.bfloat16)


def mm(left, right):
    return jnp.dot(left, right, preferred_element_type=jnp.float32)


def mm_nt(left, right):
    return lax.dot_general(left, right, (((1,), (1,)), ((), ())), preferred_element_type=jnp.float32)


def three(product, left, right):
    (lh, ll), (rh, rl) = split(left), split(right)
    return product(lh, rh) + product(lh, rl) + product(ll, rh)


def wide_left(value):
    high, low = split(value)
    return jnp.concatenate(
        [jnp.concatenate([high, high], axis=1), jnp.concatenate([low, low], axis=1)], axis=0
    )


def tall_right(value):
    return jnp.concatenate(split(value), axis=0)


def fold_halves(both):
    many = both.shape[0] // 2
    return both[:many] + both[many:]


def mm4(left, right):
    return fold_halves(mm(left, right))


def kernel(
    sizes, start_ref, len_ref, reflect_hbm, factor_hbm, panel_hbm, eig_ref, out_hbm, *scratch
):
    n, nc, sweeps, owned, blocks, band, width, rows, slices = sizes
    half = band // 2
    chunks = eig_ref.shape[1] // LANES
    per_group = chunks // GROUPS
    group_cols = per_group * LANES
    slice_rows = band // slices
    first, middle_end = 2 * half, 2 * half + rows

    count = (sweeps + 1) * GROUPS
    exts, scratch = scratch[:count], scratch[count:]
    (reflect_ref, factor_ref, panel_ref, early, load_sem, packed, pt, gram_out, gram_in, gram_full, proj_out, proj_in, proj_full,
     up_out, up_in, down_out, down_in, known_up, known_down,
     head_out, head_in, tail_out, tail_in, corner_sems, weights, weight_sems, out_ref, out_sems,
     eig_sem, up_send, up_recv, down_send, down_recv,
     right_send, left_send, piece_recv, sum_sems) = scratch

    me = lax.axis_index("row")
    z = lax.axis_index("col")

    def ext(t, g):
        return exts[t * GROUPS + g]

    barrier = pltpu.get_barrier_semaphore()
    for k in range(1, n):
        pl.semaphore_signal(barrier, inc=1, device_id={"row": lax.rem(me + k, n)}, device_id_type=MESH)

    @pl.when(z > 0)
    def _():
        pl.semaphore_signal(barrier, inc=1, device_id={"col": z - 1}, device_id_type=MESH)

    @pl.when(z < nc - 1)
    def _():
        pl.semaphore_signal(barrier, inc=1, device_id={"col": z + 1}, device_id_type=MESH)


    block_loads = [
        pltpu.make_async_copy(reflect_hbm, reflect_ref, load_sem.at[0]),
        pltpu.make_async_copy(factor_hbm, factor_ref, load_sem.at[1]),
    ]
    panel_load = pltpu.make_async_copy(panel_hbm, panel_ref.at[half:half + rows], load_sem.at[2])
    for copy in block_loads:
        copy.start()
    loads = []
    for c in range(chunks):
        g, i = divmod(c, per_group)
        copy = pltpu.make_async_copy(
            eig_ref.at[:, c * LANES:(c + 1) * LANES],
            ext(0, g).at[i, first:middle_end],
            eig_sem.at[c],
        )
        copy.start()
        loads.append(copy)
    panel_load.start()

    flat_row = lax.broadcasted_iota(jnp.int32, (width, band), 0)
    flat_col = lax.broadcasted_iota(jnp.int32, (width, band), 1)
    right_of = flat_col > flat_row
    unit = (flat_col == flat_row).astype(jnp.float32)
    for copy in block_loads:
        copy.wait()
    for i in range(owned):
        for b in range(blocks):
            turned = jnp.transpose(factor_ref[i, b])
            turned = jnp.concatenate([turned, jnp.zeros((width, band - width), jnp.float32)], axis=1)
            packed[z * owned + i, b] = jnp.where(right_of, reflect_ref[i, b], turned)

    zeros = jnp.zeros((half, LANES), jnp.float32)
    turns = sweeps // 2 + 1

    @pl.when(me == 0)
    def _():
        panel_ref[:half] = zeros
        weights[:half] = zeros
        tail_in[...] = jnp.zeros_like(tail_in)
        for t in range(sweeps + 1):
            for g in range(GROUPS):
                for i in range(per_group):
                    ext(t, g)[i, :half] = zeros
                    if t == 0:
                        ext(t, g)[i, half:first] = zeros

    @pl.when(me == n - 1)
    def _():
        panel_ref[half + rows:] = zeros
        weights[middle_end:middle_end + half] = zeros
        head_in[...] = jnp.zeros_like(head_in)
        for turn in range(turns):
            for g in range(GROUPS):
                for i in range(per_group):
                    up_in[turn, g, i] = zeros

    inside = jnp.logical_and(z > 0, z < nc - 1)

    @pl.when(inside)
    def _():
        pl.semaphore_wait(barrier, n - 1 + 2)

    @pl.when(jnp.logical_not(inside))
    def _():
        pl.semaphore_wait(barrier, n - 1 + min(1, nc - 1))


    def piece(s, b, to_right):
        sems = right_send if to_right else left_send
        return pltpu.make_async_remote_copy(
            packed.at[s, b], packed.at[s, b], sems.at[s, b], piece_recv.at[s, b],
            device_id={"col": z + 1 if to_right else z - 1}, device_id_type=MESH,
        )

    def send_own(i, to_right):
        for b in range(blocks):
            piece_copy = pltpu.make_async_remote_copy(
                packed.at[z * owned + i, b], packed.at[z * owned + i, b],
                (right_send if to_right else left_send).at[z * owned + i, b],
                piece_recv.at[z * owned + i, b],
                device_id={"col": z + 1 if to_right else z - 1}, device_id_type=MESH,
            )
            piece_copy.start()

    @pl.when(z == 0)
    def _():
        for i in range(owned):
            send_own(i, True)

    @pl.when(jnp.logical_and(z > 0, z < nc - 1))
    def _():
        send_own(0, True)

    @pl.when(jnp.logical_and(z >= nc - 2, z < nc - 1))
    def _():
        for i in range(1, owned):
            send_own(i, True)

    @pl.when(z > 0)
    def _():
        for i in range(owned):
            send_own(i, False)

    forwards = {}
    waited_early = {}
    for s in range(sweeps):
        origin = s // owned
        for where in range(origin + 1, nc - 1):
            step = 0 if s < owned else s - 1
            forwards.setdefault(step, []).append((s, where, True))
            waited_early.setdefault(s, []).append(where)
        for where in range(1, origin):
            step = min(s, s % owned + 1 + owned * (origin - where - 1))
            forwards.setdefault(step, []).append((s, where, False))
            waited_early.setdefault(s, []).append(where)

    def gather_step(t):
        for s, where, to_right in forwards.get(t, []):
            @pl.when(z == where)
            def _():
                for b in range(blocks):
                    copy = piece(s, b, to_right)
                    copy.wait_recv()
                    copy.start()
        if t % 2 == 1:
            mine = (t + 1) // 2
            if mine < nc - 2:
                @pl.when(z == mine)
                def _():
                    for i in range(1, owned):
                        send_own(i, True)
        keep = z != t // owned
        for where in waited_early.get(t, []):
            keep = jnp.logical_and(keep, z != where)

        @pl.when(keep)
        def _():
            for b in range(blocks):
                pltpu.make_async_copy(packed.at[t, b], packed.at[t, b], piece_recv.at[t, b]).wait()

    def finish_gather():
        for s in range(sweeps):
            origin = s // owned

            @pl.when(jnp.logical_and(z >= origin, z < nc - 1))
            def _():
                for b in range(blocks):
                    piece(s, b, True).wait_send()

            @pl.when(jnp.logical_and(z <= origin, z > 0))
            def _():
                for b in range(blocks):
                    piece(s, b, False).wait_send()

    def up_copy(t, g):
        turn = (t + 1) // 2
        source = ext(0, g).at[:, first:first + half] if t == 0 else up_out.at[turn, g]
        return pltpu.make_async_remote_copy(
            source, up_in.at[turn, g],
            up_send.at[turn, g], up_recv.at[turn, g], device_id={"row": me - 1}, device_id_type=MESH,
        )

    def down_copy(t, g):
        turn = (t + 1) // 2
        return pltpu.make_async_remote_copy(
            down_out.at[turn, g], down_in.at[turn, g],
            down_send.at[turn, g], down_recv.at[turn, g], device_id={"row": me + 1}, device_id_type=MESH,
        )

    def head_copy(t):
        turn = (t + 1) // 2
        return pltpu.make_async_remote_copy(
            head_out.at[turn], head_in.at[turn], corner_sems.at[turn, 0], corner_sems.at[turn, 1],
            device_id={"row": me - 1}, device_id_type=MESH,
        )

    def tail_copy(t):
        turn = (t + 1) // 2
        return pltpu.make_async_remote_copy(
            tail_out.at[turn], tail_in.at[turn], corner_sems.at[turn, 2], corner_sems.at[turn, 3],
            device_id={"row": me + 1}, device_id_type=MESH,
        )

    def halo_start(t, g):
        @pl.when(me > 0)
        def _():
            up_copy(t, g).start()
        if t > 0:
            @pl.when(me < n - 1)
            def _():
                down_copy(t, g).start()

    def halo_take(t, g):
        turn = (t + 1) // 2
        here = ext(t, g)

        @pl.when(me < n - 1)
        def _():
            up_copy(t, g).wait_recv()

        for i in range(per_group):
            here[i, middle_end:middle_end + half] = up_in[turn, g, i]
        if t > 0:
            @pl.when(me > 0)
            def _():
                down_copy(t, g).wait_recv()
                for i in range(per_group):
                    here[i, half:first] = down_in[turn, g, i]

    def finish_halo():
        for t in [0] + list(range(1, sweeps, 2)):
            for g in range(GROUPS):
                @pl.when(me > 0)
                def _():
                    up_copy(t, g).wait_send()
                if t > 0:
                    @pl.when(me < n - 1)
                    def _():
                        down_copy(t, g).wait_send()
            if t > 0:
                if t < sweeps - 1:
                    @pl.when(me > 0)
                    def _():
                        head_copy(t).wait_send()

                @pl.when(me < n - 1)
                def _():
                    tail_copy(t).wait_send()

    def owner_only(owner, run):
        if slices == n:
            run()
        else:
            pl.when(owner < slices)(run)

    def owners_differ(refs, sem):
        def wait(many):
            view = refs.at[pl.ds(0, many)]
            pltpu.make_async_copy(view, view, sem).wait()

        if slices == n:
            wait(slices - 1)
        else:
            pl.when(me < slices)(lambda: wait(slices - 1))
            pl.when(me >= slices)(lambda: wait(slices))

    def scatter_start(out, into, base):
        for k in range(1, n):
            peer = lax.rem(me + k, n)

            def run():
                pltpu.make_async_remote_copy(
                    out.at[peer], into.at[n - k - 1], sum_sems.at[base], sum_sems.at[base + 1],
                    device_id={"row": peer}, device_id_type=MESH,
                ).start()

            owner_only(peer, run)

    def reduce_and_spread(out, into, full, base):
        def run():
            pltpu.make_async_copy(into, into, sum_sems.at[base + 1]).wait()
            total = out[me]
            for k in range(n - 1):
                total = total + into[k]
            full[me] = total
            for k in range(1, n):
                pltpu.make_async_remote_copy(
                    full.at[me], full.at[me], sum_sems.at[base + 2], sum_sems.at[base + 3],
                    device_id={"row": lax.rem(me + k, n)}, device_id_type=MESH,
                ).start()

        owner_only(me, run)

    def spread_wait(full, base):
        owners_differ(full, sum_sems.at[base + 3])

    def finish_sum(out, into, base):
        owners_differ(out, sum_sems.at[base])

        def run():
            pltpu.make_async_copy(into, into, sum_sems.at[base + 2]).wait()

        owner_only(me, run)

    for copy in loads:
        copy.wait()
    for g in range(GROUPS):
        halo_start(0, g)

    panel_load.wait()
    panel_up = pltpu.make_async_remote_copy(
        panel_ref.at[half:2 * half], panel_ref.at[half + rows:2 * half + rows],
        load_sem.at[3], load_sem.at[4], device_id={"row": me - 1}, device_id_type=MESH,
    )

    @pl.when(me > 0)
    def _():
        panel_up.start()

    highest = lax.Precision.HIGHEST
    row_id = lax.broadcasted_iota(jnp.int32, (band, band), 0)
    col_id = lax.broadcasted_iota(jnp.int32, (band, band), 1)
    identity = (row_id == col_id).astype(jnp.float32)
    state = {}

    def factor_start():
        spread_wait(gram_full, 0)
        total = jnp.concatenate([gram_full[k] for k in range(slices)], axis=0)
        diagonal = 0.5 * total * identity
        state["by_col"] = jnp.sum(diagonal, axis=0, keepdims=True)
        by_row = jnp.sum(diagonal, axis=1, keepdims=True)
        state["power"] = jnp.where(row_id < col_id, total, 0.0) / by_row
        state["inverse"] = identity - state["power"]
        state["reach"] = 1

    def factor_more():
        if state["reach"] * 2 < band:
            state["power"] = jnp.dot(
                state["power"], state["power"], precision=highest, preferred_element_type=jnp.float32
            )
            state["inverse"] = jnp.dot(
                state["inverse"], identity + state["power"],
                precision=highest, preferred_element_type=jnp.float32,
            )
            state["reach"] *= 2

    def offset(t):
        return start_ref[t] if 0 <= t < sweeps else 0

    def delta(t):
        return offset(t) - offset(t - 1)

    def take(ref, at, many):
        return jnp.concatenate([ref[i, pl.ds(at, many), :] for i in range(per_group)], axis=1)

    def put(ref, at, value):
        for i in range(per_group):
            ref[i, at:at + value.shape[0]] = value[:, i * LANES:(i + 1) * LANES]

    band_row = lax.broadcasted_iota(jnp.int32, (band, group_cols), 0)
    half_row = lax.broadcasted_iota(jnp.int32, (half, group_cols), 0)
    squares = {}
    corners = {}

    weight_up = pltpu.make_async_remote_copy(
        weights.at[first:first + half], weights.at[middle_end:middle_end + half],
        weight_sems.at[0], weight_sems.at[1], device_id={"row": me - 1}, device_id_type=MESH,
    )
    weight_down = pltpu.make_async_remote_copy(
        weights.at[middle_end - half:middle_end], weights.at[half:first],
        weight_sems.at[2], weight_sems.at[3], device_id={"row": me + 1}, device_id_type=MESH,
    )

    def weights_take():
        @pl.when(me < n - 1)
        def _():
            weight_up.wait_recv()

        @pl.when(me > 0)
        def _():
            weight_down.wait_recv()

        for b in range(blocks):
            early[b] = wide_left(
                jnp.transpose(weights[pl.ds(first + b * band - delta(sweeps - 1), band), :])
            )

    def project(g):
        here = ext(sweeps - 1, g)
        total = mm4(early[0], tall_right(take(here, first, band)))
        for b in range(1, blocks):
            total = total + mm4(early[b], tall_right(take(here, first + b * band, band)))
        for k in range(slices):
            proj_out[g, k] = total[k * slice_rows:(k + 1) * slice_rows]

        @pl.when(me == 0)
        def _():
            side = jnp.transpose(weights[pl.ds(first - half - delta(sweeps - 1), half), :])
            more = three(mm, side, take(here, half, half))
            for k in range(slices):
                proj_out[g, k] = proj_out[g, k] + more[k * slice_rows:(k + 1) * slice_rows]

        scatter_start(proj_out.at[g], proj_in.at[g], 4 + 4 * g)

    def prepare(t):
        gather_step(t)
        plain = []
        squares[t] = []
        for b in range(blocks):
            pack = packed[t, b]
            flat = jnp.where(right_of, pack, unit)
            flat = jnp.where(flat_col < len_ref[b, t], flat, 0.0)
            turned = jnp.where(right_of, 0.0, pack)[:, :width]
            scaled = fold_halves(mm_nt(wide_left(jnp.transpose(flat)), jnp.concatenate(split(turned), axis=1)))
            square = mm4(wide_left(scaled), tall_right(flat))
            plain.append(square)
            squares[t].append(wide_left(square))
            if t == sweeps - 1:
                if b == 0:
                    @pl.when(me < n - 1)
                    def _():
                        panel_up.wait_recv()
                side = panel_ref[pl.ds(half + b * band + start_ref[t], band), :]
                weights[first + b * band:first + (b + 1) * band] = side - mm4(
                    wide_left(jnp.transpose(square)), tall_right(side)
                )
        if t == sweeps - 1:
            @pl.when(me == 0)
            def _():
                weights[half:first] = panel_ref[pl.ds(start_ref[t], half), :]

            @pl.when(me > 0)
            def _():
                weight_up.start()

            @pl.when(me < n - 1)
            def _():
                weight_down.start()
        if t % 2 == 1:
            turn = (t + 1) // 2
            quarter = half // 2

            def fold(corner):
                return jnp.concatenate([corner[:quarter], corner[quarter:]], axis=1)

            if t < sweeps - 1:
                head_out[turn] = fold((identity - plain[0])[:half, :half])

                @pl.when(me > 0)
                def _():
                    head_copy(t).start()
            tail_out[turn] = fold((identity - plain[-1])[half:, half:])

            @pl.when(me < n - 1)
            def _():
                tail_copy(t).start()

    def corner_take(t):
        turn = (t + 1) // 2

        def unfold(both):
            return wide_left(jnp.concatenate([both[:, :half], both[:, half:]], axis=0))

        if t < sweeps - 1:
            @pl.when(me < n - 1)
            def _():
                head_copy(t).wait_recv()
            corners[t, 0] = unfold(head_in[turn])

        @pl.when(me > 0)
        def _():
            tail_copy(t).wait_recv()
        corners[t, 1] = unfold(tail_in[turn])

    def part(wide, at):
        return jnp.concatenate([wide[at:at + half], wide[band + at:band + at + half]], axis=0)

    def send_ahead(t, g):
        turn = (t + 1) // 2
        here = ext(t, g)
        move = delta(t)
        down_by, up_by = jnp.maximum(move, 0), jnp.maximum(-move, 0)
        top = take(here, first, half)
        if t < sweeps - 1:
            window = take(here, first + move, band)
            window = jnp.where(band_row + move >= 0, window, 0.0)
            put(known_up.at[g], half, window[:half] - mm4(part(squares[t][0], 0), tall_right(window)))
            top = jnp.where(half_row < down_by, top, take(known_up.at[g], half - down_by, half))
        put(up_out.at[turn, g], 0, top)
        window = take(here, first + (blocks - 1) * band + move, band)
        window = jnp.where(band_row + move < band, window, 0.0)
        put(known_down.at[g], 0, window[half:] - mm4(part(squares[t][-1], half), tall_right(window)))
        low = jnp.where(
            half_row >= half - up_by, take(here, middle_end - half, half), take(known_down.at[g], up_by, half)
        )
        put(down_out.at[turn, g], 0, low)
        halo_start(t, g)

    def sweep(t, g):
        here, after = ext(t, g), ext(t + 1, g)
        move = delta(t)
        for b in range(blocks):
            window = take(here, first + b * band + move, band)
            put(after, first + b * band, window - mm4(squares[t][b], tall_right(window)))
        if t % 2 == 1:
            shift = jnp.where(me == 0, move, jnp.minimum(move, 0))
            lead = jnp.where(half_row >= half - move, take(here, first + move - half, half), 0.0)
            put(after, half, take(here, half + shift, half) + mm4(corners[t, 1], tall_right(lead)))
            if t < sweeps - 1:
                rest = jnp.where(half_row < -move, take(here, middle_end + move, half), 0.0)
                put(
                    after, middle_end,
                    take(here, middle_end + jnp.maximum(move, 0), half) + mm4(corners[t, 0], tall_right(rest)),
                )
        else:
            @pl.when(me == 0)
            def _():
                put(after, half, take(here, half + move, half))

    def gram_start():
        transposed = jnp.transpose(panel_ref[half:half + rows])
        for b in range(blocks):
            pt[b] = wide_left(transposed[:, b * band:(b + 1) * band])
        gram = mm4(pt[0], tall_right(panel_ref[half:half + band]))
        for b in range(1, blocks):
            gram = gram + mm4(pt[b], tall_right(panel_ref[half + b * band:half + (b + 1) * band]))
        for k in range(slices):
            gram_out[k] = gram[k * slice_rows:(k + 1) * slice_rows]
        scatter_start(gram_out, gram_in, 0)

    prepare(0)
    for g in range(GROUPS):
        halo_take(0, g)
        sweep(0, g)
    prepare(1)
    for g in range(GROUPS):
        send_ahead(1, g)
    gram_start()
    prepare(2)
    for t in range(1, sweeps, 2):
        if t + 1 < sweeps:
            prepare(t + 2)
        corner_take(t)
        for g in range(GROUPS):
            halo_take(t, g)
            sweep(t, g)
            if t + 1 < sweeps:
                sweep(t + 1, g)
                send_ahead(t + 2, g)
        if t + 1 == sweeps:
            for g in range(GROUPS):
                reduce_and_spread(proj_out.at[g], proj_in.at[g], proj_full.at[g], 4 + 4 * g)
        if t + 3 == sweeps:
            weights_take()
            for g in range(GROUPS):
                project(g)
        if t == 1:
            reduce_and_spread(gram_out, gram_in, gram_full, 0)
        if t == 3:
            factor_start()
        if 3 <= t < sweeps - 1:
            for _ in range(4):
                factor_more()
        if t + 3 < sweeps:
            prepare(t + 3)

    for g in range(GROUPS):
        columns = slice(g * group_cols, (g + 1) * group_cols)
        here = ext(sweeps, g)
        for b in range(blocks):
            out_ref[b * band:(b + 1) * band, columns] = take(here, first + b * band + delta(sweeps), band)
    while state["reach"] * 2 < band:
        factor_more()

    factor = wide_left(state["inverse"] / state["by_col"])
    inner = []
    for g in range(GROUPS):
        spread_wait(proj_full.at[g], 4 + 4 * g)
        projection = jnp.concatenate([proj_full[g, k] for k in range(slices)], axis=0)
        inner.append(tall_right(mm4(factor, tall_right(projection))))
    stores = []
    for b in range(blocks):
        span = slice(b * band, (b + 1) * band)
        side = wide_left(panel_ref[half + b * band:half + (b + 1) * band])
        for g in range(GROUPS):
            columns = slice(g * group_cols, (g + 1) * group_cols)
            out_ref[span, columns] = out_ref[span, columns] - mm4(side, inner[g])
        store = pltpu.make_async_copy(out_ref.at[span], out_hbm.at[span], out_sems.at[b])
        store.start()
        stores.append(store)

    @pl.when(me > 0)
    def _():
        panel_up.wait_send()
        weight_up.wait_send()

    @pl.when(me < n - 1)
    def _():
        weight_down.wait_send()

    finish_gather()
    finish_halo()
    for store in stores:
        store.wait()
    finish_sum(gram_out, gram_in, 0)
    for g in range(GROUPS):
        finish_sum(proj_out.at[g], proj_in.at[g], 4 + 4 * g)


def body(sweep_start, block_len, reflectors, tfactors, panel, eigvecs):
    rows, cols = eigvecs.shape
    owned, blocks, band, width = reflectors.shape
    flat = jnp.swapaxes(reflectors, 2, 3)
    n, nc = lax.axis_size("row"), lax.axis_size("col")
    sweeps = owned * nc
    slices = min(n, band // 8)
    part = band // slices
    chunks = cols // LANES
    group_cols = cols // GROUPS
    turns = sweeps // 2 + 1
    sizes = (n, nc, sweeps, owned, blocks, band, width, rows, slices)
    vmem = pl.BlockSpec(memory_space=pltpu.VMEM)
    smem = pl.BlockSpec(memory_space=pltpu.SMEM)
    f32 = jnp.float32
    dma = pltpu.SemaphoreType.DMA
    scratch = [
        pltpu.VMEM((chunks // GROUPS, rows + 4 * (band // 2), LANES), f32)
        for _ in range((sweeps + 1) * GROUPS)
    ] + [
        pltpu.VMEM((owned, blocks, width, band), f32),
        pltpu.VMEM((owned, blocks, width, width), f32),
        pltpu.VMEM((rows + 2 * (band // 2), band), f32),
        pltpu.VMEM((blocks, 2 * band, 2 * band), jnp.bfloat16),
        dma((5,)),
        pltpu.VMEM((sweeps, blocks, width, 2 * width), f32),
        pltpu.VMEM((blocks, 2 * band, 2 * band), jnp.bfloat16),
        pltpu.VMEM((slices, part, band), f32),
        pltpu.VMEM((n - 1, part, band), f32),
        pltpu.VMEM((slices, part, band), f32),
        pltpu.VMEM((GROUPS, slices, part, group_cols), f32),
        pltpu.VMEM((GROUPS, n - 1, part, group_cols), f32),
        pltpu.VMEM((GROUPS, slices, part, group_cols), f32),
        pltpu.VMEM((turns, GROUPS, chunks // GROUPS, band // 2, LANES), f32),
        pltpu.VMEM((turns, GROUPS, chunks // GROUPS, band // 2, LANES), f32),
        pltpu.VMEM((turns, GROUPS, chunks // GROUPS, band // 2, LANES), f32),
        pltpu.VMEM((turns, GROUPS, chunks // GROUPS, band // 2, LANES), f32),
        pltpu.VMEM((GROUPS, chunks // GROUPS, band, LANES), f32),
        pltpu.VMEM((GROUPS, chunks // GROUPS, band, LANES), f32),
        pltpu.VMEM((turns, band // 4, band), f32),
        pltpu.VMEM((turns, band // 4, band), f32),
        pltpu.VMEM((turns, band // 4, band), f32),
        pltpu.VMEM((turns, band // 4, band), f32),
        dma((turns, 4)),
        pltpu.VMEM((rows + 4 * (band // 2), band), f32),
        dma((4,)),
        pltpu.VMEM((rows, cols), f32),
        dma((blocks,)),
        dma((chunks,)),
        dma((turns, GROUPS)),
        dma((turns, GROUPS)),
        dma((turns, GROUPS)),
        dma((turns, GROUPS)),
        dma((sweeps, blocks)),
        dma((sweeps, blocks)),
        dma((sweeps, blocks)),
        dma((4 + 4 * GROUPS,)),
    ]
    return pl.pallas_call(
        functools.partial(kernel, sizes),
        out_shape=jax.ShapeDtypeStruct((rows, cols), f32),
        in_specs=[smem, smem] + [pl.BlockSpec(memory_space=pl.ANY)] * 4,
        out_specs=pl.BlockSpec(memory_space=pl.ANY),
        scratch_shapes=scratch,
        compiler_params=pltpu.CompilerParams(
            collective_id=0, has_side_effects=True, vmem_limit_bytes=65_900_000
        ),
    )(sweep_start, block_len.T, flat, tfactors, panel, eigvecs)


def solution(mesh):
    in_specs = (
        P(),
        P(None, "row"),
        P("col", "row", None, None),
        P("col", "row", None, None),
        P("row", None),
        P("row", "col"),
    )
    return jax.shard_map(body, mesh=mesh, in_specs=in_specs, out_specs=P("row", "col"), check_vma=False)
```

```python
import functools

import jax
import jax.numpy as jnp
from jax import lax
from jax.experimental import pallas as pl
from jax.experimental.pallas import tpu as pltpu
from jax.sharding import PartitionSpec as P

MESH = pl.DeviceIdType.MESH
LANES = 128
GROUPS = 2


def split(value):
    high = value.astype(jnp.bfloat16)
    return high, (value - high.astype(jnp.float32)).astype(jnp.bfloat16)


def mm(left, right):
    return jnp.dot(left, right, preferred_element_type=jnp.float32)


def mm_nt(left, right):
    return lax.dot_general(left, right, (((1,), (1,)), ((), ())), preferred_element_type=jnp.float32)


def three(product, left, right):
    (lh, ll), (rh, rl) = split(left), split(right)
    return product(lh, rh) + product(lh, rl) + product(ll, rh)


def wide_left(value):
    high, low = split(value)
    return jnp.concatenate(
        [jnp.concatenate([high, high], axis=1), jnp.concatenate([low, low], axis=1)], axis=0
    )


def tall_right(value):
    return jnp.concatenate(split(value), axis=0)


def fold_halves(both):
    many = both.shape[0] // 2
    return both[:many] + both[many:]


def mm4(left, right):
    return fold_halves(mm(left, right))


def kernel(
    sizes, start_ref, len_ref, reflect_hbm, factor_hbm, panel_hbm, eig_ref, out_hbm, *scratch
):
    n, nc, sweeps, owned, blocks, band, width, rows, slices = sizes
    half = band // 2
    chunks = eig_ref.shape[1] // LANES
    per_group = chunks // GROUPS
    group_cols = per_group * LANES
    slice_rows = band // slices
    first, middle_end = 2 * half, 2 * half + rows

    count = (sweeps + 1) * GROUPS
    exts, scratch = scratch[:count], scratch[count:]
    (reflect_ref, factor_ref, panel_ref, early, load_sem, packed, pt, gram_out, gram_in, gram_full, proj_out, proj_in, proj_full,
     up_out, up_in, down_out, down_in, known_up, known_down,
     head_out, head_in, tail_out, tail_in, corner_sems, weights, weight_sems, out_ref, out_sems,
     eig_sem, up_send, up_recv, down_send, down_recv,
     right_send, left_send, piece_recv, sum_sems) = scratch

    me = lax.axis_index("row")
    z = lax.axis_index("col")

    def ext(t, g):
        return exts[t * GROUPS + g]

    barrier = pltpu.get_barrier_semaphore()
    for k in range(1, n):
        pl.semaphore_signal(barrier, inc=1, device_id={"row": lax.rem(me + k, n)}, device_id_type=MESH)

    @pl.when(z > 0)
    def _():
        pl.semaphore_signal(barrier, inc=1, device_id={"col": z - 1}, device_id_type=MESH)

    @pl.when(z < nc - 1)
    def _():
        pl.semaphore_signal(barrier, inc=1, device_id={"col": z + 1}, device_id_type=MESH)


    block_loads = [
        pltpu.make_async_copy(reflect_hbm, reflect_ref, load_sem.at[0]),
        pltpu.make_async_copy(factor_hbm, factor_ref, load_sem.at[1]),
    ]
    panel_load = pltpu.make_async_copy(panel_hbm, panel_ref.at[half:half + rows], load_sem.at[2])
    for copy in block_loads:
        copy.start()
    loads = []
    for c in range(chunks):
        g, i = divmod(c, per_group)
        copy = pltpu.make_async_copy(
            eig_ref.at[:, c * LANES:(c + 1) * LANES],
            ext(0, g).at[i, first:middle_end],
            eig_sem.at[c],
        )
        copy.start()
        loads.append(copy)
    panel_load.start()

    flat_row = lax.broadcasted_iota(jnp.int32, (width, band), 0)
    flat_col = lax.broadcasted_iota(jnp.int32, (width, band), 1)
    right_of = flat_col > flat_row
    unit = (flat_col == flat_row).astype(jnp.float32)
    for copy in block_loads:
        copy.wait()
    for i in range(owned):
        for b in range(blocks):
            turned = jnp.transpose(factor_ref[i, b])
            turned = jnp.concatenate([turned, jnp.zeros((width, band - width), jnp.float32)], axis=1)
            packed[z * owned + i, b] = jnp.where(right_of, reflect_ref[i, b], turned)

    zeros = jnp.zeros((half, LANES), jnp.float32)
    turns = sweeps // 2 + 1

    @pl.when(me == 0)
    def _():
        panel_ref[:half] = zeros
        weights[:half] = zeros
        tail_in[...] = jnp.zeros_like(tail_in)
        for t in range(sweeps + 1):
            for g in range(GROUPS):
                for i in range(per_group):
                    ext(t, g)[i, :half] = zeros
                    if t == 0:
                        ext(t, g)[i, half:first] = zeros

    @pl.when(me == n - 1)
    def _():
        panel_ref[half + rows:] = zeros
        weights[middle_end:middle_end + half] = zeros
        head_in[...] = jnp.zeros_like(head_in)
        for turn in range(turns):
            for g in range(GROUPS):
                for i in range(per_group):
                    up_in[turn, g, i] = zeros

    inside = jnp.logical_and(z > 0, z < nc - 1)

    @pl.when(inside)
    def _():
        pl.semaphore_wait(barrier, n - 1 + 2)

    @pl.when(jnp.logical_not(inside))
    def _():
        pl.semaphore_wait(barrier, n - 1 + min(1, nc - 1))


    def piece(s, b, to_right):
        sems = right_send if to_right else left_send
        return pltpu.make_async_remote_copy(
            packed.at[s, b], packed.at[s, b], sems.at[s, b], piece_recv.at[s, b],
            device_id={"col": z + 1 if to_right else z - 1}, device_id_type=MESH,
        )

    def send_own(i, to_right):
        for b in range(blocks):
            piece_copy = pltpu.make_async_remote_copy(
                packed.at[z * owned + i, b], packed.at[z * owned + i, b],
                (right_send if to_right else left_send).at[z * owned + i, b],
                piece_recv.at[z * owned + i, b],
                device_id={"col": z + 1 if to_right else z - 1}, device_id_type=MESH,
            )
            piece_copy.start()

    @pl.when(z == 0)
    def _():
        for i in range(owned):
            send_own(i, True)

    @pl.when(jnp.logical_and(z > 0, z < nc - 1))
    def _():
        send_own(0, True)

    @pl.when(jnp.logical_and(z >= nc - 2, z < nc - 1))
    def _():
        for i in range(1, owned):
            send_own(i, True)

    @pl.when(z > 0)
    def _():
        for i in range(owned):
            send_own(i, False)

    forwards = {}
    waited_early = {}
    for s in range(sweeps):
        origin = s // owned
        for where in range(origin + 1, nc - 1):
            step = 0 if s < owned else s - 1
            forwards.setdefault(step, []).append((s, where, True))
            waited_early.setdefault(s, []).append(where)
        for where in range(1, origin):
            step = min(s, s % owned + 1 + owned * (origin - where - 1))
            forwards.setdefault(step, []).append((s, where, False))
            waited_early.setdefault(s, []).append(where)

    def gather_step(t):
        for s, where, to_right in forwards.get(t, []):
            @pl.when(z == where)
            def _():
                for b in range(blocks):
                    copy = piece(s, b, to_right)
                    copy.wait_recv()
                    copy.start()
        if t % 2 == 1:
            mine = (t + 1) // 2
            if mine < nc - 2:
                @pl.when(z == mine)
                def _():
                    for i in range(1, owned):
                        send_own(i, True)
        keep = z != t // owned
        for where in waited_early.get(t, []):
            keep = jnp.logical_and(keep, z != where)

        @pl.when(keep)
        def _():
            for b in range(blocks):
                pltpu.make_async_copy(packed.at[t, b], packed.at[t, b], piece_recv.at[t, b]).wait()

    def finish_gather():
        for s in range(sweeps):
            origin = s // owned

            @pl.when(jnp.logical_and(z >= origin, z < nc - 1))
            def _():
                for b in range(blocks):
                    piece(s, b, True).wait_send()

            @pl.when(jnp.logical_and(z <= origin, z > 0))
            def _():
                for b in range(blocks):
                    piece(s, b, False).wait_send()

    def up_copy(t, g):
        turn = (t + 1) // 2
        source = ext(0, g).at[:, first:first + half] if t == 0 else up_out.at[turn, g]
        return pltpu.make_async_remote_copy(
            source, up_in.at[turn, g],
            up_send.at[turn, g], up_recv.at[turn, g], device_id={"row": me - 1}, device_id_type=MESH,
        )

    def down_copy(t, g):
        turn = (t + 1) // 2
        return pltpu.make_async_remote_copy(
            down_out.at[turn, g], down_in.at[turn, g],
            down_send.at[turn, g], down_recv.at[turn, g], device_id={"row": me + 1}, device_id_type=MESH,
        )

    def head_copy(t):
        turn = (t + 1) // 2
        return pltpu.make_async_remote_copy(
            head_out.at[turn], head_in.at[turn], corner_sems.at[turn, 0], corner_sems.at[turn, 1],
            device_id={"row": me - 1}, device_id_type=MESH,
        )

    def tail_copy(t):
        turn = (t + 1) // 2
        return pltpu.make_async_remote_copy(
            tail_out.at[turn], tail_in.at[turn], corner_sems.at[turn, 2], corner_sems.at[turn, 3],
            device_id={"row": me + 1}, device_id_type=MESH,
        )

    def halo_start(t, g):
        @pl.when(me > 0)
        def _():
            up_copy(t, g).start()
        if t > 0:
            @pl.when(me < n - 1)
            def _():
                down_copy(t, g).start()

    def halo_take(t, g):
        turn = (t + 1) // 2
        here = ext(t, g)

        @pl.when(me < n - 1)
        def _():
            up_copy(t, g).wait_recv()

        for i in range(per_group):
            here[i, middle_end:middle_end + half] = up_in[turn, g, i]
        if t > 0:
            @pl.when(me > 0)
            def _():
                down_copy(t, g).wait_recv()
                for i in range(per_group):
                    here[i, half:first] = down_in[turn, g, i]

    def finish_halo():
        for t in [0] + list(range(1, sweeps, 2)):
            for g in range(GROUPS):
                @pl.when(me > 0)
                def _():
                    up_copy(t, g).wait_send()
                if t > 0:
                    @pl.when(me < n - 1)
                    def _():
                        down_copy(t, g).wait_send()
            if t > 0:
                if t < sweeps - 1:
                    @pl.when(me > 0)
                    def _():
                        head_copy(t).wait_send()

                @pl.when(me < n - 1)
                def _():
                    tail_copy(t).wait_send()

    def owner_only(owner, run):
        if slices == n:
            run()
        else:
            pl.when(owner < slices)(run)

    def owners_differ(refs, sem):
        def wait(many):
            view = refs.at[pl.ds(0, many)]
            pltpu.make_async_copy(view, view, sem).wait()

        if slices == n:
            wait(slices - 1)
        else:
            pl.when(me < slices)(lambda: wait(slices - 1))
            pl.when(me >= slices)(lambda: wait(slices))

    def scatter_start(out, into, base):
        for k in range(1, n):
            peer = lax.rem(me + k, n)

            def run():
                pltpu.make_async_remote_copy(
                    out.at[peer], into.at[n - k - 1], sum_sems.at[base], sum_sems.at[base + 1],
                    device_id={"row": peer}, device_id_type=MESH,
                ).start()

            owner_only(peer, run)

    def reduce_and_spread(out, into, full, base):
        def run():
            pltpu.make_async_copy(into, into, sum_sems.at[base + 1]).wait()
            total = out[me]
            for k in range(n - 1):
                total = total + into[k]
            full[me] = total
            for k in range(1, n):
                pltpu.make_async_remote_copy(
                    full.at[me], full.at[me], sum_sems.at[base + 2], sum_sems.at[base + 3],
                    device_id={"row": lax.rem(me + k, n)}, device_id_type=MESH,
                ).start()

        owner_only(me, run)

    def spread_wait(full, base):
        owners_differ(full, sum_sems.at[base + 3])

    def finish_sum(out, into, base):
        owners_differ(out, sum_sems.at[base])

        def run():
            pltpu.make_async_copy(into, into, sum_sems.at[base + 2]).wait()

        owner_only(me, run)

    for copy in loads:
        copy.wait()
    for g in range(GROUPS):
        halo_start(0, g)

    panel_load.wait()
    panel_up = pltpu.make_async_remote_copy(
        panel_ref.at[half:2 * half], panel_ref.at[half + rows:2 * half + rows],
        load_sem.at[3], load_sem.at[4], device_id={"row": me - 1}, device_id_type=MESH,
    )

    @pl.when(me > 0)
    def _():
        panel_up.start()

    highest = lax.Precision.HIGHEST
    row_id = lax.broadcasted_iota(jnp.int32, (band, band), 0)
    col_id = lax.broadcasted_iota(jnp.int32, (band, band), 1)
    identity = (row_id == col_id).astype(jnp.float32)
    state = {}

    def factor_start():
        spread_wait(gram_full, 0)
        total = jnp.concatenate([gram_full[k] for k in range(slices)], axis=0)
        diagonal = 0.5 * total * identity
        state["by_col"] = jnp.sum(diagonal, axis=0, keepdims=True)
        by_row = jnp.sum(diagonal, axis=1, keepdims=True)
        state["power"] = jnp.where(row_id < col_id, total, 0.0) / by_row
        state["inverse"] = identity - state["power"]
        state["reach"] = 1

    def factor_more():
        if state["reach"] * 2 < band:
            state["power"] = jnp.dot(
                state["power"], state["power"], precision=highest, preferred_element_type=jnp.float32
            )
            state["inverse"] = jnp.dot(
                state["inverse"], identity + state["power"],
                precision=highest, preferred_element_type=jnp.float32,
            )
            state["reach"] *= 2

    def offset(t):
        return start_ref[t] if 0 <= t < sweeps else 0

    def delta(t):
        return offset(t) - offset(t - 1)

    def take(ref, at, many):
        return jnp.concatenate([ref[i, pl.ds(at, many), :] for i in range(per_group)], axis=1)

    def put(ref, at, value):
        for i in range(per_group):
            ref[i, at:at + value.shape[0]] = value[:, i * LANES:(i + 1) * LANES]

    band_row = lax.broadcasted_iota(jnp.int32, (band, group_cols), 0)
    half_row = lax.broadcasted_iota(jnp.int32, (half, group_cols), 0)
    squares = {}
    corners = {}

    weight_up = pltpu.make_async_remote_copy(
        weights.at[first:first + half], weights.at[middle_end:middle_end + half],
        weight_sems.at[0], weight_sems.at[1], device_id={"row": me - 1}, device_id_type=MESH,
    )
    weight_down = pltpu.make_async_remote_copy(
        weights.at[middle_end - half:middle_end], weights.at[half:first],
        weight_sems.at[2], weight_sems.at[3], device_id={"row": me + 1}, device_id_type=MESH,
    )

    def weights_take():
        @pl.when(me < n - 1)
        def _():
            weight_up.wait_recv()

        @pl.when(me > 0)
        def _():
            weight_down.wait_recv()

        for b in range(blocks):
            early[b] = wide_left(
                jnp.transpose(weights[pl.ds(first + b * band - delta(sweeps - 1), band), :])
            )

    def project(g):
        here = ext(sweeps - 1, g)
        total = mm4(early[0], tall_right(take(here, first, band)))
        for b in range(1, blocks):
            total = total + mm4(early[b], tall_right(take(here, first + b * band, band)))
        for k in range(slices):
            proj_out[g, k] = total[k * slice_rows:(k + 1) * slice_rows]

        @pl.when(me == 0)
        def _():
            side = jnp.transpose(weights[pl.ds(first - half - delta(sweeps - 1), half), :])
            more = three(mm, side, take(here, half, half))
            for k in range(slices):
                proj_out[g, k] = proj_out[g, k] + more[k * slice_rows:(k + 1) * slice_rows]

        scatter_start(proj_out.at[g], proj_in.at[g], 4 + 4 * g)

    def prepare(t):
        gather_step(t)
        plain = []
        squares[t] = []
        for b in range(blocks):
            pack = packed[t, b]
            flat = jnp.where(right_of, pack, unit)
            flat = jnp.where(flat_col < len_ref[b, t], flat, 0.0)
            turned = jnp.where(right_of, 0.0, pack)[:, :width]
            scaled = fold_halves(mm_nt(wide_left(jnp.transpose(flat)), jnp.concatenate(split(turned), axis=1)))
            square = mm4(wide_left(scaled), tall_right(flat))
            plain.append(square)
            squares[t].append(wide_left(square))
            if t == sweeps - 1:
                if b == 0:
                    @pl.when(me < n - 1)
                    def _():
                        panel_up.wait_recv()
                side = panel_ref[pl.ds(half + b * band + start_ref[t], band), :]
                weights[first + b * band:first + (b + 1) * band] = side - mm4(
                    wide_left(jnp.transpose(square)), tall_right(side)
                )
        if t == sweeps - 1:
            @pl.when(me == 0)
            def _():
                weights[half:first] = panel_ref[pl.ds(start_ref[t], half), :]

            @pl.when(me > 0)
            def _():
                weight_up.start()

            @pl.when(me < n - 1)
            def _():
                weight_down.start()
        if t % 2 == 1:
            turn = (t + 1) // 2
            quarter = half // 2

            def fold(corner):
                return jnp.concatenate([corner[:quarter], corner[quarter:]], axis=1)

            if t < sweeps - 1:
                head_out[turn] = fold((identity - plain[0])[:half, :half])

                @pl.when(me > 0)
                def _():
                    head_copy(t).start()
            tail_out[turn] = fold((identity - plain[-1])[half:, half:])

            @pl.when(me < n - 1)
            def _():
                tail_copy(t).start()

    def corner_take(t):
        turn = (t + 1) // 2

        def unfold(both):
            return wide_left(jnp.concatenate([both[:, :half], both[:, half:]], axis=0))

        if t < sweeps - 1:
            @pl.when(me < n - 1)
            def _():
                head_copy(t).wait_recv()
            corners[t, 0] = unfold(head_in[turn])

        @pl.when(me > 0)
        def _():
            tail_copy(t).wait_recv()
        corners[t, 1] = unfold(tail_in[turn])

    def part(wide, at):
        return jnp.concatenate([wide[at:at + half], wide[band + at:band + at + half]], axis=0)

    def send_ahead(t, g):
        turn = (t + 1) // 2
        here = ext(t, g)
        move = delta(t)
        down_by, up_by = jnp.maximum(move, 0), jnp.maximum(-move, 0)
        top = take(here, first, half)
        if t < sweeps - 1:
            window = take(here, first + move, band)
            window = jnp.where(band_row + move >= 0, window, 0.0)
            put(known_up.at[g], half, window[:half] - mm4(part(squares[t][0], 0), tall_right(window)))
            top = jnp.where(half_row < down_by, top, take(known_up.at[g], half - down_by, half))
        put(up_out.at[turn, g], 0, top)
        window = take(here, first + (blocks - 1) * band + move, band)
        window = jnp.where(band_row + move < band, window, 0.0)
        put(known_down.at[g], 0, window[half:] - mm4(part(squares[t][-1], half), tall_right(window)))
        low = jnp.where(
            half_row >= half - up_by, take(here, middle_end - half, half), take(known_down.at[g], up_by, half)
        )
        put(down_out.at[turn, g], 0, low)
        halo_start(t, g)

    def sweep(t, g):
        here, after = ext(t, g), ext(t + 1, g)
        move = delta(t)
        for b in range(blocks):
            window = take(here, first + b * band + move, band)
            put(after, first + b * band, window - mm4(squares[t][b], tall_right(window)))
        if t % 2 == 1:
            shift = jnp.where(me == 0, move, jnp.minimum(move, 0))
            lead = jnp.where(half_row >= half - move, take(here, first + move - half, half), 0.0)
            put(after, half, take(here, half + shift, half) + mm4(corners[t, 1], tall_right(lead)))
            if t < sweeps - 1:
                rest = jnp.where(half_row < -move, take(here, middle_end + move, half), 0.0)
                put(
                    after, middle_end,
                    take(here, middle_end + jnp.maximum(move, 0), half) + mm4(corners[t, 0], tall_right(rest)),
                )
        else:
            @pl.when(me == 0)
            def _():
                put(after, half, take(here, half + move, half))

    def gram_start():
        transposed = jnp.transpose(panel_ref[half:half + rows])
        for b in range(blocks):
            pt[b] = wide_left(transposed[:, b * band:(b + 1) * band])
        gram = mm4(pt[0], tall_right(panel_ref[half:half + band]))
        for b in range(1, blocks):
            gram = gram + mm4(pt[b], tall_right(panel_ref[half + b * band:half + (b + 1) * band]))
        for k in range(slices):
            gram_out[k] = gram[k * slice_rows:(k + 1) * slice_rows]
        scatter_start(gram_out, gram_in, 0)

    prepare(0)
    for g in range(GROUPS):
        halo_take(0, g)
        sweep(0, g)
    prepare(1)
    for g in range(GROUPS):
        send_ahead(1, g)
    prepare(2)
    gram_start()

    for t in range(1, sweeps, 2):
        if t + 1 < sweeps:
            prepare(t + 2)
        corner_take(t)
        for g in range(GROUPS):
            halo_take(t, g)
            sweep(t, g)
            if t + 1 < sweeps:
                sweep(t + 1, g)
                send_ahead(t + 2, g)
        if t + 1 == sweeps:
            for g in range(GROUPS):
                reduce_and_spread(proj_out.at[g], proj_in.at[g], proj_full.at[g], 4 + 4 * g)
        if t + 3 == sweeps:
            weights_take()
            for g in range(GROUPS):
                project(g)
        if t == 1:
            reduce_and_spread(gram_out, gram_in, gram_full, 0)
        if t == 3:
            factor_start()
        if 3 <= t < sweeps - 1:
            for _ in range(4):
                factor_more()
        if t + 3 < sweeps:
            prepare(t + 3)

    for g in range(GROUPS):
        columns = slice(g * group_cols, (g + 1) * group_cols)
        here = ext(sweeps, g)
        for b in range(blocks):
            out_ref[b * band:(b + 1) * band, columns] = take(here, first + b * band + delta(sweeps), band)
    while state["reach"] * 2 < band:
        factor_more()

    factor = wide_left(state["inverse"] / state["by_col"])
    inner = []
    for g in range(GROUPS):
        spread_wait(proj_full.at[g], 4 + 4 * g)
        projection = jnp.concatenate([proj_full[g, k] for k in range(slices)], axis=0)
        inner.append(tall_right(mm4(factor, tall_right(projection))))
    stores = []
    for b in range(blocks):
        span = slice(b * band, (b + 1) * band)
        side = wide_left(panel_ref[half + b * band:half + (b + 1) * band])
        for g in range(GROUPS):
            columns = slice(g * group_cols, (g + 1) * group_cols)
            out_ref[span, columns] = out_ref[span, columns] - mm4(side, inner[g])
        store = pltpu.make_async_copy(out_ref.at[span], out_hbm.at[span], out_sems.at[b])
        store.start()
        stores.append(store)

    @pl.when(me > 0)
    def _():
        panel_up.wait_send()
        weight_up.wait_send()

    @pl.when(me < n - 1)
    def _():
        weight_down.wait_send()

    finish_gather()
    finish_halo()
    for store in stores:
        store.wait()
    finish_sum(gram_out, gram_in, 0)
    for g in range(GROUPS):
        finish_sum(proj_out.at[g], proj_in.at[g], 4 + 4 * g)


def body(sweep_start, block_len, reflectors, tfactors, panel, eigvecs):
    rows, cols = eigvecs.shape
    owned, blocks, band, width = reflectors.shape
    flat = jnp.swapaxes(reflectors, 2, 3)
    n, nc = lax.axis_size("row"), lax.axis_size("col")
    sweeps = owned * nc
    slices = min(n, band // 8)
    part = band // slices
    chunks = cols // LANES
    group_cols = cols // GROUPS
    turns = sweeps // 2 + 1
    sizes = (n, nc, sweeps, owned, blocks, band, width, rows, slices)
    vmem = pl.BlockSpec(memory_space=pltpu.VMEM)
    smem = pl.BlockSpec(memory_space=pltpu.SMEM)
    f32 = jnp.float32
    dma = pltpu.SemaphoreType.DMA
    scratch = [
        pltpu.VMEM((chunks // GROUPS, rows + 4 * (band // 2), LANES), f32)
        for _ in range((sweeps + 1) * GROUPS)
    ] + [
        pltpu.VMEM((owned, blocks, width, band), f32),
        pltpu.VMEM((owned, blocks, width, width), f32),
        pltpu.VMEM((rows + 2 * (band // 2), band), f32),
        pltpu.VMEM((blocks, 2 * band, 2 * band), jnp.bfloat16),
        dma((5,)),
        pltpu.VMEM((sweeps, blocks, width, 2 * width), f32),
        pltpu.VMEM((blocks, 2 * band, 2 * band), jnp.bfloat16),
        pltpu.VMEM((slices, part, band), f32),
        pltpu.VMEM((n - 1, part, band), f32),
        pltpu.VMEM((slices, part, band), f32),
        pltpu.VMEM((GROUPS, slices, part, group_cols), f32),
        pltpu.VMEM((GROUPS, n - 1, part, group_cols), f32),
        pltpu.VMEM((GROUPS, slices, part, group_cols), f32),
        pltpu.VMEM((turns, GROUPS, chunks // GROUPS, band // 2, LANES), f32),
        pltpu.VMEM((turns, GROUPS, chunks // GROUPS, band // 2, LANES), f32),
        pltpu.VMEM((turns, GROUPS, chunks // GROUPS, band // 2, LANES), f32),
        pltpu.VMEM((turns, GROUPS, chunks // GROUPS, band // 2, LANES), f32),
        pltpu.VMEM((GROUPS, chunks // GROUPS, band, LANES), f32),
        pltpu.VMEM((GROUPS, chunks // GROUPS, band, LANES), f32),
        pltpu.VMEM((turns, band // 4, band), f32),
        pltpu.VMEM((turns, band // 4, band), f32),
        pltpu.VMEM((turns, band // 4, band), f32),
        pltpu.VMEM((turns, band // 4, band), f32),
        dma((turns, 4)),
        pltpu.VMEM((rows + 4 * (band // 2), band), f32),
        dma((4,)),
        pltpu.VMEM((rows, cols), f32),
        dma((blocks,)),
        dma((chunks,)),
        dma((turns, GROUPS)),
        dma((turns, GROUPS)),
        dma((turns, GROUPS)),
        dma((turns, GROUPS)),
        dma((sweeps, blocks)),
        dma((sweeps, blocks)),
        dma((sweeps, blocks)),
        dma((4 + 4 * GROUPS,)),
    ]
    return pl.pallas_call(
        functools.partial(kernel, sizes),
        out_shape=jax.ShapeDtypeStruct((rows, cols), f32),
        in_specs=[smem, smem] + [pl.BlockSpec(memory_space=pl.ANY)] * 4,
        out_specs=pl.BlockSpec(memory_space=pl.ANY),
        scratch_shapes=scratch,
        compiler_params=pltpu.CompilerParams(
            collective_id=0, has_side_effects=True, vmem_limit_bytes=65_900_000
        ),
    )(sweep_start, block_len.T, flat, tfactors, panel, eigvecs)


def solution(mesh):
    in_specs = (
        P(),
        P(None, "row"),
        P("col", "row", None, None),
        P("col", "row", None, None),
        P("row", None),
        P("row", "col"),
    )
    return jax.shard_map(body, mesh=mesh, in_specs=in_specs, out_specs=P("row", "col"), check_vma=False)
```
